32 devices in a mesh: row: 4 (over y, x), col: 8 (over z, core).
Axes of the slice: x: 2, y: 2, z: 4, core: 2. Of those that a mesh axis runs over, the one named last changes fastest.
Arguments:
- trailing: float32 [3072, 3072], P('row', 'col'), may hold values from -6 to 6, as said below
- v_panels: bfloat16 [3, 3072, 256], P(None, ('row', 'col')), may hold values from -6 to 6
Outputs:
- updated: float32 [3072, 3072], P('row', 'col')
- w_panels: float32 [3, 3072, 256], P(None, ('row', 'col'))
The draws below stay inside these ranges and needn't reach their ends.
Inputs may be any that keep to these rules, and one draw needn't show every extreme that they name: trailing is symmetric: entry (i, j) equals entry (j, i).
All inputs are finite; a program needn't handle non-finite values.
Results may differ from the reference program's by a relative error of at most 0.0003.
Values may be sent and summed in bfloat16 or wider, within the bound.
A program may use at most 64 MiB of HBM per device.

```python
import math
import jax
import jax.numpy as jnp
from jax import lax

K = 256
TICKS = 3
ORDER = 3072


def draw_trailing(key, part):
    base = jax.random.normal(jax.random.fold_in(key, 11), (ORDER, ORDER), jnp.float32)
    mirrored = (base + base.T) * 0.7071067811865476
    return jnp.clip(mirrored, -6.0, 6.0)


def steps_of(rng, dims, pieces, smallest, largest):
    gain = 1.0
    for axis_at, shards_of in pieces:
        draws = jax.random.uniform(jax.random.fold_in(jax.random.fold_in(rng, 6), axis_at), (shards_of,), jnp.float32, smallest / len(pieces), largest / len(pieces))
        gain = gain * jnp.repeat(jnp.exp(draws), dims[axis_at] // shards_of).reshape((-1,) + (1,) * (len(dims) - 1 - axis_at))
    return gain


def scatter_about(stream_key, dims, deviation, reach, cuts=(), held_as=jnp.bfloat16):
    result = deviation * jax.random.normal(stream_key, dims, jnp.float32)
    if cuts:
        result = result * steps_of(stream_key, dims, cuts, -0.22, 0.18)
    return jnp.clip(result, -reach, reach).astype(held_as)


def setup_inputs(seed: int = 0) -> dict:
    splits = jax.random.split(jax.random.key(seed), 3)
    trailing = draw_trailing(jax.random.fold_in(splits[2], 71), 0)
    v_panels = scatter_about(splits[1], (TICKS, ORDER, K), 1.0, 6.0, ((1, 32),))
    return dict(trailing=trailing, v_panels=v_panels)


def reference(trailing, v_panels):
    scaling = 1.0 / math.sqrt(ORDER)
    current = trailing
    w_list = []
    for tick in range(TICKS):
        v_now = v_panels[tick].astype(jnp.float32)
        product = jnp.dot(current, v_now, precision=lax.Precision.HIGHEST, preferred_element_type=jnp.float32)
        w_now = product * scaling
        rows_side = jnp.concatenate([v_now, w_now], axis=1)
        cols_side = jnp.concatenate([w_now, v_now], axis=1)
        update = lax.dot_general(rows_side, cols_side, (((1,), (1,)), ((), ())), precision=lax.Precision.HIGHEST, preferred_element_type=jnp.float32)
        current = current - update * (0.5 * scaling)
        w_list.append(w_now)
    return (current, jnp.stack(w_list, axis=0))
```

```python
import functools
import math

import jax
import jax.numpy as jnp
from jax import lax
from jax.experimental import pallas as pl
from jax.experimental.pallas import tpu as pltpu
from jax.sharding import PartitionSpec as P

MESH = pl.DeviceIdType.MESH
NT = (((1,), (1,)), ((), ()))
NN = (((1,), (0,)), ((), ()))
TN = (((0,), (0,)), ((), ()))
SPAN = 124.0
TINY = 1e-30
TILE = 16


def dot(a, b, dims):
    return lax.dot_general(a, b, dims, preferred_element_type=jnp.float32)


def halves(x):
    high = x.astype(jnp.bfloat16)
    return high, (x - high.astype(jnp.float32)).astype(jnp.bfloat16)


def dot2(a, b, dims):
    return dot(a[0], b[0], dims) + (dot(a[0], b[1], dims) + dot(a[1], b[0], dims))


def encode(ref, x):
    rows = x.shape[0]
    peak = jnp.maximum(jnp.max(jnp.abs(x), axis=0, keepdims=True), TINY).astype(jnp.bfloat16)
    ref[pl.ds(0, rows)] = jnp.exp2(x * (SPAN / peak.astype(jnp.float32))).astype(jnp.bfloat16)
    ref[pl.ds(ref.shape[0] - TILE, TILE)] = jnp.broadcast_to(peak, (TILE, x.shape[1]))


def decode(ref, rows):
    peak = ref[pl.ds(ref.shape[0] - TILE, TILE)].astype(jnp.float32)[:1]
    return jnp.log2(ref[pl.ds(0, rows)].astype(jnp.float32)) * (peak * (1.0 / SPAN))


def kernel(
    nrow, ncol, ratio, scaling,
    a_ref, v_ref, out_ref, w_ref,
    b_ref, vr, vt, part, sent, got, wcc, wrc, wc, wr, gp, ga, gb, gc, full,
    v_send, v_recv, vt_send, vt_recv, vx_send, vx_recv,
    rs_send, rs_recv, wc_send, wc_recv, wr_send, wr_recv, local_sem,
    ga_send, ga_recv, gb_send, gb_recv, gc_send, gc_recv, gd_send, gd_recv, ge_send, ge_recv,
):
    ticks, piece, depth = v_ref.shape
    rows_tile, cols_tile = a_ref.shape
    links = ncol // ratio
    pairs = full.shape[1]
    r = lax.axis_index("row")
    c = lax.axis_index("col")
    q = c // ratio
    j = c % ratio
    half = 0.5 * scaling
    share = depth // ratio
    slot = share // links

    def rows(at):
        return pl.ds(pl.multiple_of(at * piece, piece), piece)

    def remote(src, dst, send, recv, row, col):
        return pltpu.make_async_remote_copy(
            src_ref=src, dst_ref=dst, send_sem=send, recv_sem=recv,
            device_id=(row, col), device_id_type=MESH,
        )

    from_row, from_col = c // ratio, j * nrow + r
    to_row, to_col = c % nrow, r * ratio + c // nrow
    stays = jnp.logical_and(to_row == r, to_col == c)

    barrier = pltpu.get_barrier_semaphore()
    for i in range(1, nrow):
        pl.semaphore_signal(barrier, inc=1, device_id=((r + i) % nrow, c), device_id_type=MESH)
    for i in range(1, ncol):
        pl.semaphore_signal(barrier, inc=1, device_id=(r, (c + i) % ncol), device_id_type=MESH)

    @pl.when(jnp.logical_not(stays))
    def _():
        pl.semaphore_signal(barrier, inc=1, device_id=(from_row, from_col), device_id_type=MESH)
        pl.semaphore_signal(barrier, inc=1, device_id=(to_row, to_col), device_id_type=MESH)

    pl.semaphore_wait(barrier, nrow + ncol - 2 + jnp.where(stays, 0, 2))

    def v_out(t, i):
        return remote(
            v_ref.at[t], vr.at[t, rows(c)], v_send.at[t, i], v_recv.at[t, c],
            r, ((q + i) % links) * ratio + j,
        )

    def v_side(t, i, k):
        src_col = ((q + i) % links) * ratio + j
        src = v_ref.at[t] if i == 0 else vr.at[t, rows(src_col)]
        return remote(
            src, vr.at[t, rows(src_col)], vx_send.at[t, i, k - 1], v_recv.at[t, src_col],
            r, q * ratio + (j + k) % ratio,
        )

    def v_own(t):
        return pltpu.make_async_copy(v_ref.at[t], vr.at[t, rows(c)], v_recv.at[t, c])

    def v_in(t, col):
        return pltpu.make_async_copy(v_ref.at[t], vr.at[t, rows(col)], v_recv.at[t, col])

    def v_start(t):
        for i in range(1, links):
            v_out(t, i).start()
        for k in range(1, ratio):
            v_side(t, 0, k).start()
        v_own(t).start()

    vt_move = remote(v_ref, vt.at[:, rows(to_row)], vt_send, vt_recv, to_row, to_col)
    vt_in = pltpu.make_async_copy(v_ref, vt.at[:, rows(r)], vt_recv)

    v_start(0)

    @pl.when(stays)
    def _():
        vt_in.start()

    @pl.when(jnp.logical_not(stays))
    def _():
        vt_move.start()

    for t in range(1, ticks):
        v_start(t)

    b_ref[0], b_ref[1] = halves(a_ref[...].T)

    def v_relay(t):
        for i in range(1, links):
            v_in(t, ((q + i) % links) * ratio + j).wait()
            for k in range(1, ratio):
                v_side(t, i, k).start()

    def v_finish(t):
        v_in(t, c).wait()
        for i in range(links):
            for k in range(1, ratio):
                v_in(t, ((q + i) % links) * ratio + (j + k) % ratio).wait()

    def rs_out(t, i):
        peer = (r + i) % nrow
        return remote(
            sent.at[t, peer], got.at[t, r], rs_send.at[t, i], rs_recv.at[t, r], peer, c
        )

    def rs_in(t, peer):
        return pltpu.make_async_copy(sent.at[t, peer], got.at[t, peer], rs_recv.at[t, peer])

    def wc_out(t, i):
        peer = (r + i) % nrow
        spot = wcc.at[t, r]
        return remote(spot, spot, wc_send.at[t, i], wc_recv.at[t, r], peer, c)

    def wc_in(t, peer):
        spot = wcc.at[t, peer]
        return pltpu.make_async_copy(spot, spot, wc_recv.at[t, peer])

    def vt_out(t, i):
        peer = (r + i) % nrow
        spot = vt.at[t, rows(r)]
        return remote(spot, spot, vx_send.at[t, links + i - 1, 0], vx_recv.at[t, r], peer, c)

    def vt_got(t, peer):
        spot = vt.at[t, rows(peer)]
        return pltpu.make_async_copy(spot, spot, vx_recv.at[t, peer])

    source = q == r
    up = jnp.logical_and(q >= r, q < links - 1)
    down = jnp.logical_and(q <= r, q > 0)

    def wr_out(t, i, way, first):
        peer = (r + i) % nrow
        at = j * nrow + peer
        spot = wrc.at[t, at]
        src = wcc.at[t, peer] if first else spot
        if way == 0:
            col = c + ratio
        elif way == 1:
            col = c - ratio
        else:
            col = q * ratio + (j + way - 1) % ratio
        return remote(src, spot, wr_send.at[t, i, way], wr_recv.at[t, at], r, col)

    def wr_in(t, seat, peer):
        at = seat * nrow + peer
        spot = wrc.at[t, at]
        return pltpu.make_async_copy(spot, spot, wr_recv.at[t, at])

    def wr_keep(t, i):
        peer = (r + i) % nrow
        return pltpu.make_async_copy(
            wcc.at[t, peer], wrc.at[t, j * nrow + peer], local_sem.at[t, i]
        )

    def wr_ways(t, i, first, act):
        @pl.when(up)
        def _():
            act(wr_out(t, i, 0, first))

        @pl.when(down)
        def _():
            act(wr_out(t, i, 1, first))

        for k in range(1, ratio):
            act(wr_out(t, i, 1 + k, first))

    def start(copy):
        copy.start()

    def wait_send(copy):
        copy.wait_send()

    def partial(t):
        v_relay(t)
        v_finish(t)
        part[t] = dot(b_ref[0], vr[t], NN) + dot(b_ref[1], vr[t], NN)
        for i in range(1, nrow):
            peer = (r + i) % nrow
            encode(sent.at[t, peer], part[t, rows(peer)])
            rs_out(t, i).start()

    def collect(t):
        total = part[t, rows(r)]
        for i in range(1, nrow):
            peer = (r + i) % nrow
            rs_in(t, peer).wait()
            total = total + decode(got.at[t, peer], piece)
        encode(wcc.at[t, r], total * scaling)
        for i in range(1, nrow):
            wc_out(t, i).start()

        @pl.when(source)
        def _():
            wr_ways(t, 0, True, start)
            wr_keep(t, 0).start()

    def relay(t):
        @pl.when(source)
        def _():
            for i in range(1, nrow):
                wc_in(t, (r + i) % nrow).wait()
                wr_ways(t, i, True, start)
                wr_keep(t, i).start()

        @pl.when(jnp.logical_not(source))
        def _():
            for i in range(nrow):
                wr_in(t, j, (r + i) % nrow).wait()
                wr_ways(t, i, False, start)
            for i in range(1, nrow):
                wc_in(t, (r + i) % nrow).wait()

    def open_cols(t):
        for k in range(nrow):
            wc[t, 0, pl.ds(k * piece, piece)], wc[t, 1, pl.ds(k * piece, piece)] = halves(
                decode(wcc.at[t, k], piece)
            )

    def open_rows(t):
        @pl.when(source)
        def _():
            for i in range(nrow):
                wr_keep(t, i).wait()

        for k in range(1, ratio):
            for i in range(nrow):
                wr_in(t, (j + k) % ratio, (r + i) % nrow).wait()
        for k in range(ratio * nrow):
            wr[t, 0, pl.ds(k * piece, piece)], wr[t, 1, pl.ds(k * piece, piece)] = halves(
                decode(wrc.at[t, k], piece)
            )

    owner = r < pairs
    first = r // 2
    later = (r + 3) // 2

    def shares(at):
        return pl.ds(pl.multiple_of(at * share, share), share)

    def slots(at):
        return pl.ds(pl.multiple_of(at * slot, slot), slot)

    def ga_out(k, s):
        to = (j + s) % ratio
        return remote(
            gp.at[k, shares(to)], ga.at[k, j], ga_send.at[k, s], ga_recv.at[k, j],
            r, q * ratio + to,
        )

    def ga_in(k, s):
        at = (j + s) % ratio
        return pltpu.make_async_copy(ga.at[k, at], ga.at[k, at], ga_recv.at[k, at])

    def gb_out(k, s):
        to = (q + s) % links
        return remote(
            gb.at[k, slots(to)], gc.at[k, q], gb_send.at[k, s], gb_recv.at[k, q],
            r, to * ratio + j,
        )

    def gb_in(k, s):
        at = (q + s) % links
        return pltpu.make_async_copy(gc.at[k, at], gc.at[k, at], gb_recv.at[k, at])

    def final(k, at):
        return full.at[k, r, pl.ds(pl.multiple_of(j * share + at * slot, slot), slot)]

    def gc_out(k, s):
        to = (q + s) % links
        return remote(
            final(k, q), final(k, q), gc_send.at[k, s], gc_recv.at[k, q], r, to * ratio + j
        )

    def gc_in(k, s):
        at = (q + s) % links
        return pltpu.make_async_copy(final(k, at), final(k, at), gc_recv.at[k, at])

    def gd_out(k, i):
        spot = full.at[k, r, shares(j)]
        return remote(spot, spot, gd_send.at[k, i], gd_recv.at[k, r], (r + i) % nrow, c)

    def gd_in(k, m):
        spot = full.at[k, m, shares(j)]
        return pltpu.make_async_copy(spot, spot, gd_recv.at[k, m])

    def ge_out(k, s):
        spot = full.at[k, :, shares(j)]
        return remote(
            spot, spot, ge_send.at[k, s], ge_recv.at[k, j], r, q * ratio + (j + s) % ratio
        )

    def ge_in(k, s):
        at = (j + s) % ratio
        spot = full.at[k, :, shares(at)]
        return pltpu.make_async_copy(spot, spot, ge_recv.at[k, at])

    def gram_a(k):
        @pl.when(owner)
        def _():
            if k:
                gp[k] = dot(wc[first, 0], vt[later], TN) + dot(wc[first, 1], vt[later], TN)
            else:
                gp[k] = dot(vt[first], vt[later], TN)
            for s in range(1, ratio):
                ga_out(k, s).start()

    def gram_b(k):
        @pl.when(owner)
        def _():
            total = gp[k, shares(j)]
            for s in range(1, ratio):
                ga_in(k, s).wait()
                total = total + ga[k, (j + s) % ratio]
            gb[k] = total
            for s in range(1, links):
                gb_out(k, s).start()

    def gram_c(k):
        @pl.when(owner)
        def _():
            total = gb[k, slots(q)]
            for s in range(1, links):
                gb_in(k, s).wait()
                total = total + gc[k, (q + s) % links]
            full[k, r, pl.ds(pl.multiple_of(j * share + q * slot, slot), slot)] = total
            for s in range(1, links):
                gc_out(k, s).start()

    def gram_d(k):
        @pl.when(owner)
        def _():
            for s in range(1, links):
                gc_in(k, s).wait()
            for i in range(1, nrow):
                gd_out(k, i).start()

    def gram_e(k):
        for m in range(pairs):
            @pl.when(r != m)
            def _():
                gd_in(k, m).wait()
        for s in range(1, ratio):
            ge_out(k, s).start()

    def gram_f(k):
        for s in range(1, ratio):
            ge_in(k, s).wait()

    partial(0)
    partial(1)

    @pl.when(stays)
    def _():
        vt_in.wait()

    @pl.when(jnp.logical_not(stays))
    def _():
        vt_move.wait()

    for t in range(ticks):
        for i in range(1, nrow):
            vt_out(t, i).start()

    collect(0)
    partial(2)
    collect(1)
    relay(0)
    for t in range(ticks):
        for i in range(1, nrow):
            vt_got(t, (r + i) % nrow).wait()
    gram_a(0)
    open_cols(0)
    collect(2)
    gram_b(0)
    relay(1)
    open_cols(1)
    gram_a(1)
    gram_c(0)
    gram_b(1)
    gram_d(0)
    open_rows(0)

    def update(t):
        out_ref[...] = (out_ref if t else a_ref)[...] - half * (
            dot(vr[t], wc[t, 0], NT) + dot(vr[t], wc[t, 1], NT)
            + dot(wr[t, 0], vt[t], NT) + dot(wr[t, 1], vt[t], NT)
        )

    gram_c(1)
    relay(2)
    gram_e(0)
    gram_d(1)
    update(0)
    open_rows(1)
    open_cols(2)
    gram_f(0)
    gram_e(1)
    gram_f(1)
    fix = scaling * half
    g01, g02, g12 = (halves(full[0, m]) for m in range(3))
    n01, n02 = (halves(full[1, m]) for m in range(2))
    k12 = halves(full[1, 2] - fix * (dot2(n01, g02, TN) + dot2(g01, n02, TN)))

    def one(v, x):
        base = x[1, 0].astype(jnp.float32) + x[1, 1].astype(jnp.float32)
        return base - fix * (
            dot(v[0], n01[0], NN) + dot(v[0], n01[1], NN)
            + dot2((x[0, 0], x[0, 1]), g01, NN)
        )

    def two(v, x):
        base = x[2, 0].astype(jnp.float32) + x[2, 1].astype(jnp.float32)
        return base - fix * (
            dot(v[0], n02[0], NN) + dot(v[0], n02[1], NN)
            + dot2((x[0, 0], x[0, 1]), g02, NN)
            + dot(v[1], k12[0], NN) + dot(v[1], k12[1], NN)
            + dot2((x[1, 0], x[1, 1]), g12, NN)
        )

    wc[1, 0], wc[1, 1] = halves(one(vt, wc))
    wr[1, 0], wr[1, 1] = halves(one(vr, wr))
    update(1)
    wc[2, 0], wc[2, 1] = halves(two(vt, wc))
    open_rows(2)
    wr[2, 0], wr[2, 1] = halves(two(vr, wr))
    update(2)
    mine = rows(c)
    for t in range(ticks):
        w_ref[t] = wr[t, 0, mine].astype(jnp.float32) + wr[t, 1, mine].astype(jnp.float32)

    for t in range(ticks):
        for i in range(1, links):
            v_out(t, i).wait_send()
        for i in range(links):
            for k in range(1, ratio):
                v_side(t, i, k).wait_send()
        for i in range(1, nrow):
            vt_out(t, i).wait_send()
            rs_out(t, i).wait_send()
            wc_out(t, i).wait_send()

        @pl.when(source)
        def _():
            for i in range(nrow):
                wr_ways(t, i, True, wait_send)

        @pl.when(jnp.logical_not(source))
        def _():
            for i in range(nrow):
                wr_ways(t, i, False, wait_send)

    for k in range(2):
        @pl.when(owner)
        def _():
            for s in range(1, ratio):
                ga_out(k, s).wait_send()
            for s in range(1, links):
                gb_out(k, s).wait_send()
                gc_out(k, s).wait_send()
            for i in range(1, nrow):
                gd_out(k, i).wait_send()

        for s in range(1, ratio):
            ge_out(k, s).wait_send()


def on_device(trailing, v_panels):
    nrow = lax.axis_size("row")
    ncol = lax.axis_size("col")
    rows_tile, cols_tile = trailing.shape
    ticks, piece, depth = v_panels.shape
    ratio = rows_tile // cols_tile
    links = ncol // ratio
    scaling = 1.0 / math.sqrt(rows_tile * nrow)
    pairs = ticks * (ticks - 1) // 2
    coded = -(-piece // TILE) * TILE + TILE
    share = depth // ratio
    dma = pltpu.SemaphoreType.DMA
    vmem = pl.BlockSpec(memory_space=pltpu.VMEM)
    f32, bf16 = jnp.float32, jnp.bfloat16
    return pl.pallas_call(
        functools.partial(kernel, nrow, ncol, ratio, scaling),
        out_shape=(
            jax.ShapeDtypeStruct(trailing.shape, f32),
            jax.ShapeDtypeStruct(v_panels.shape, f32),
        ),
        in_specs=[vmem, vmem],
        out_specs=(vmem, vmem),
        scratch_shapes=[
            pltpu.VMEM((2, cols_tile, rows_tile), bf16),
            pltpu.VMEM((ticks, rows_tile, depth), bf16),
            pltpu.VMEM((ticks, cols_tile, depth), bf16),
            pltpu.VMEM((ticks, cols_tile, depth), f32),
            pltpu.VMEM((ticks, nrow, coded, depth), bf16),
            pltpu.VMEM((ticks, nrow, coded, depth), bf16),
            pltpu.VMEM((ticks, nrow, coded, depth), bf16),
            pltpu.VMEM((ticks, ratio * nrow, coded, depth), bf16),
            pltpu.VMEM((ticks, 2, cols_tile, depth), bf16),
            pltpu.VMEM((ticks, 2, rows_tile, depth), bf16),
            pltpu.VMEM((2, depth, depth), f32),
            pltpu.VMEM((2, ratio, share, depth), f32),
            pltpu.VMEM((2, share, depth), f32),
            pltpu.VMEM((2, links, share // links, depth), f32),
            pltpu.VMEM((2, pairs, depth, depth), f32),
            dma((ticks, links)),
            dma((ticks, ncol)),
            dma,
            dma,
            dma((ticks, links + nrow, ratio)),
            dma((ticks, nrow)),
            dma((ticks, nrow)),
            dma((ticks, nrow)),
            dma((ticks, nrow)),
            dma((ticks, nrow)),
            dma((ticks, nrow, ratio + 1)),
            dma((ticks, ncol)),
            dma((ticks, nrow)),
            dma((2, ratio)), dma((2, ratio)),
            dma((2, links)), dma((2, links)),
            dma((2, links)), dma((2, links)),
            dma((2, nrow)), dma((2, nrow)),
            dma((2, ratio)), dma((2, ratio)),
        ],
        compiler_params=pltpu.CompilerParams(
            collective_id=0, has_side_effects=True, vmem_limit_bytes=48 * 1024 * 1024
        ),
    )(trailing, v_panels)


def solution(mesh):
    in_specs = (P("row", "col"), P(None, ("row", "col"), None))
    out_specs = (P("row", "col"), P(None, ("row", "col"), None))
    return jax.shard_map(
        on_device, mesh=mesh, in_specs=in_specs, out_specs=out_specs, check_vma=False
    )
```

```python
import functools
import math

import jax
import jax.numpy as jnp
from jax import lax
from jax.experimental import pallas as pl
from jax.experimental.pallas import tpu as pltpu
from jax.sharding import PartitionSpec as P

MESH = pl.DeviceIdType.MESH
NT = (((1,), (1,)), ((), ()))
NN = (((1,), (0,)), ((), ()))
TN = (((0,), (0,)), ((), ()))
SPAN = 124.0
TINY = 1e-30
TILE = 8


def dot(a, b, dims):
    return lax.dot_general(a, b, dims, preferred_element_type=jnp.float32)


def halves(x):
    high = x.astype(jnp.bfloat16)
    return high, (x - high.astype(jnp.float32)).astype(jnp.bfloat16)


def dot2(a, b, dims):
    return dot(a[0], b[0], dims) + (dot(a[0], b[1], dims) + dot(a[1], b[0], dims))


def dot3(a, b, dims):
    return dot(a, b[0], dims) + dot(a, b[1], dims)


def dot4(a, b, dims):
    return dot(a[0], b, dims) + dot(a[1], b, dims)


def encode(ref, x):
    rows = x.shape[0]
    peak = jnp.maximum(jnp.max(jnp.abs(x), axis=0, keepdims=True), TINY).astype(jnp.bfloat16)
    ref[pl.ds(0, rows)] = jnp.exp2(x * (SPAN / peak.astype(jnp.float32))).astype(jnp.bfloat16)
    ref[pl.ds(ref.shape[0] - TILE, TILE)] = jnp.broadcast_to(peak, (TILE, x.shape[1]))


def decode(ref, rows):
    peak = ref[pl.ds(ref.shape[0] - TILE, TILE)].astype(jnp.float32)[:1]
    return jnp.log2(ref[pl.ds(0, rows)].astype(jnp.float32)) * (peak * (1.0 / SPAN))


def kernel(
    nrow, ncol, ratio, scaling,
    a_hbm, v_ref, out_ref, w_ref,
    a_ref, ab, vr, vt, vtt, part, sent, got, own, wcc, wrc, wct, wr, zt, gp, ga, gs, gc, gq, gram, fact,
    v_send, v_recv, vt_send, vt_recv, vx_send, vo_send, vx_recv,
    rs_send, rs_recv, wc_send, wc_recv, wr_send, wr_recv, wx_send, wx_recv, local_sem, in_sem,
    ga_send, ga_recv, gb_send, gb_recv, gd_send, gd_recv, ge_send, ge_recv,
):
    ticks, piece, depth = v_ref.shape
    rows_tile, cols_tile = a_hbm.shape
    links = ncol // ratio
    chosen = [(u, t) for t in range(ticks) for u in range(t)]
    pairs = len(chosen)
    r = lax.axis_index("row")
    c = lax.axis_index("col")
    q = c // ratio
    j = c % ratio
    half = 0.5 * scaling
    fix = scaling * half
    strip = depth // nrow
    thin = strip // ratio

    def rows(at):
        return pl.ds(pl.multiple_of(at * piece, piece), piece)

    def strips(at):
        return pl.ds(pl.multiple_of(at * strip, strip), strip)

    def thins(at):
        return pl.ds(pl.multiple_of(at * thin, thin), thin)

    def remote(src, dst, send, recv, row, col):
        return pltpu.make_async_remote_copy(
            src_ref=src, dst_ref=dst, send_sem=send, recv_sem=recv,
            device_id=(row, col), device_id_type=MESH,
        )

    from_row, from_col = c // ratio, j * nrow + r
    to_row, to_col = c % nrow, r * ratio + c // nrow
    stays = jnp.logical_and(to_row == r, to_col == c)

    a_in = pltpu.make_async_copy(a_hbm, a_ref, in_sem.at[0])
    v_own = pltpu.make_async_copy(v_ref, vr.at[:, rows(c)], in_sem.at[1])
    v_own.start()
    a_in.start()
    barrier = pltpu.get_barrier_semaphore()

    def greet(row, col):
        pl.semaphore_signal(barrier, inc=1, device_id=(row, col), device_id_type=MESH)

    for i in range(1, nrow):
        greet((r + i) % nrow, c)
    for k in range(1, ratio):
        greet(r, q * ratio + (j + k) % ratio)
    for i in range(1, links):
        greet(r, ((q + i) % links) * ratio + j)

    @pl.when(jnp.logical_not(stays))
    def _():
        greet(from_row, from_col)
        greet(to_row, to_col)

    v_own.wait()
    pl.semaphore_wait(barrier, nrow + ratio + links - 3 + jnp.where(stays, 0, 2))

    def v_out(t, i):
        spot = vr.at[t, rows(c)]
        return remote(
            spot, spot, v_send.at[t, i], v_recv.at[t, c], r, ((q + i) % links) * ratio + j
        )

    def v_side(t, i, k):
        at = ((q + i) % links) * ratio + j
        spot = vr.at[t, rows(at)]
        return remote(
            spot, spot, vx_send.at[t, i, k - 1], v_recv.at[t, at],
            r, q * ratio + (j + k) % ratio,
        )

    def v_in(t, col):
        spot = vr.at[t, rows(col)]
        return pltpu.make_async_copy(spot, spot, v_recv.at[t, col])

    vt_move = remote(v_ref, vt.at[:, rows(to_row)], vt_send, vt_recv, to_row, to_col)
    vt_in = pltpu.make_async_copy(v_ref, vt.at[:, rows(r)], vt_recv)

    def vt_out(t, i):
        peer = (r + i) % nrow
        spot = vt.at[t, rows(r)]
        return remote(spot, spot, vo_send.at[t, i], vx_recv.at[t, r], peer, c)

    def vt_got(t, peer):
        spot = vt.at[t, rows(peer)]
        return pltpu.make_async_copy(spot, spot, vx_recv.at[t, peer])

    def v_gather(t):
        for i in range(1, links):
            v_in(t, ((q + i) % links) * ratio + j).wait()
            for k in range(1, ratio):
                v_side(t, i, k).start()
        for i in range(links):
            for k in range(1, ratio):
                v_in(t, ((q + i) % links) * ratio + (j + k) % ratio).wait()

    def vt_spread():
        @pl.when(stays)
        def _():
            vt_in.wait()

        @pl.when(jnp.logical_not(stays))
        def _():
            vt_move.wait()

        for t in range(ticks):
            for i in range(1, nrow):
                vt_out(t, i).start()

    def vt_close():
        for t in range(ticks):
            for i in range(1, nrow):
                vt_got(t, (r + i) % nrow).wait()
            vtt[t] = vt[t].astype(jnp.float32).T.astype(jnp.bfloat16)

    def rs_out(t, i):
        peer = (r + i) % nrow
        return remote(
            sent.at[t, peer], got.at[t, r], rs_send.at[t, i], rs_recv.at[t, r], peer, c
        )

    def rs_in(t, peer):
        return pltpu.make_async_copy(sent.at[t, peer], got.at[t, peer], rs_recv.at[t, peer])

    def wc_out(t, i):
        spot = wcc.at[t, r]
        return remote(spot, spot, wc_send.at[t, i], wc_recv.at[t, r], (r + i) % nrow, c)

    def wc_in(t, peer):
        spot = wcc.at[t, peer]
        return pltpu.make_async_copy(spot, spot, wc_recv.at[t, peer])

    source = q == r

    def wr_out(t, i):
        return remote(
            wcc.at[t, r], wrc.at[t, j, r], wr_send.at[t, i], wr_recv.at[t, r],
            q, ((q + i) % links) * ratio + j,
        )

    def wr_in(t, peer):
        spot = wrc.at[t, j, peer]
        return pltpu.make_async_copy(spot, spot, wr_recv.at[t, peer])

    def wr_keep(t):
        return pltpu.make_async_copy(wcc.at[t], wrc.at[t, j], local_sem.at[t])

    def wx_out(t, k):
        spot = wrc.at[t, j]
        return remote(
            spot, spot, wx_send.at[t, k], wx_recv.at[t, j], r, q * ratio + (j + k) % ratio
        )

    def wx_in(t, k):
        at = (j + k) % ratio
        spot = wrc.at[t, at]
        return pltpu.make_async_copy(spot, spot, wx_recv.at[t, at])

    def partial(t):
        v_gather(t)
        part[t] = dot(vr[t], ab[0], TN) + dot(vr[t], ab[1], TN)
        for i in range(1, nrow):
            peer = (r + i) % nrow
            encode(sent.at[t, peer], part[t, strips(peer)])
            rs_out(t, i).start()

    def collect(t):
        total = part[t, strips(r)]
        for i in range(1, nrow):
            peer = (r + i) % nrow
            rs_in(t, peer).wait()
            total = total + decode(got.at[t, peer], strip)
        total = total * scaling
        encode(wcc.at[t, r], total)
        for i in range(1, nrow):
            wc_out(t, i).start()
        for i in range(1, links):
            wr_out(t, i).start()
        own[t, 0], own[t, 1] = halves(total)

    def relay(t):
        for i in range(1, nrow):
            wc_in(t, (r + i) % nrow).wait()

        @pl.when(source)
        def _():
            wr_keep(t).start()
            wr_keep(t).wait()

        @pl.when(jnp.logical_not(source))
        def _():
            for i in range(nrow):
                wr_in(t, (r + i) % nrow).wait()

        for k in range(1, ratio):
            wx_out(t, k).start()

    def open_cols(t):
        for k in range(nrow):
            at = pl.ds(k * strip, strip)
            wct[t, 0, at], wct[t, 1, at] = halves(decode(wcc.at[t, k], strip))

    def open_rows(t):
        for k in range(1, ratio):
            wx_in(t, k).wait()
        for s in range(ratio):
            x = jnp.concatenate([decode(wrc.at[t, s, k], strip) for k in range(nrow)], axis=0)
            at = pl.ds(s * cols_tile, cols_tile)
            wr[t, 0, at], wr[t, 1, at] = halves(x.T)

    def ga_out(k, s):
        to = (j + s) % ratio
        return remote(
            gp.at[k, :, thins(to)], ga.at[k, j], ga_send.at[k, s], ga_recv.at[k, j],
            r, q * ratio + to,
        )

    def ga_in(k, s):
        at = (j + s) % ratio
        return pltpu.make_async_copy(ga.at[k, at], ga.at[k, at], ga_recv.at[k, at])

    def gb_out(k, s):
        return remote(
            gs.at[k], gc.at[k, q], gb_send.at[k, s], gb_recv.at[k, q],
            r, ((q + s) % links) * ratio + j,
        )

    def gb_in(k, s):
        at = (q + s) % links
        return pltpu.make_async_copy(gc.at[k, at], gc.at[k, at], gb_recv.at[k, at])

    def gd_out(k, i):
        spot = gq.at[k, j, r]
        return remote(spot, spot, gd_send.at[k, i], gd_recv.at[k, r], (r + i) % nrow, c)

    def gd_in(k, i):
        at = (r + i) % nrow
        spot = gq.at[k, j, at]
        return pltpu.make_async_copy(spot, spot, gd_recv.at[k, at])

    def ge_out(k, s):
        spot = gq.at[k, j]
        return remote(
            spot, spot, ge_send.at[k, s], ge_recv.at[k, j], r, q * ratio + (j + s) % ratio
        )

    def ge_in(k, s):
        at = (j + s) % ratio
        spot = gq.at[k, at]
        return pltpu.make_async_copy(spot, spot, ge_recv.at[k, at])

    def gram_a(k):
        for m, (u, t) in enumerate(chosen):
            gp[k, m] = dot4(own.at[u], vt[t], NN) if k else dot(vtt[u, strips(r)], vt[t], NN)
        for s in range(1, ratio):
            ga_out(k, s).start()

    def gram_b(k):
        for s in range(1, ratio):
            ga_in(k, s).wait()
        for m in range(pairs):
            total = gp[k, m, thins(j)]
            for s in range(1, ratio):
                total = total + ga[k, (j + s) % ratio, m]
            gp[k, m, thins(j)] = total
            encode(gs.at[k, m], total)
        for s in range(1, links):
            gb_out(k, s).start()

    def gram_d(k):
        for s in range(1, links):
            gb_in(k, s).wait()
        for m in range(pairs):
            total = gp[k, m, thins(j)]
            for s in range(1, links):
                total = total + decode(gc.at[k, (q + s) % links, m], thin)
            encode(gq.at[k, j, r, m], total)
        for i in range(1, nrow):
            gd_out(k, i).start()

    def gram_e(k):
        for i in range(1, nrow):
            gd_in(k, i).wait()
        for s in range(1, ratio):
            ge_out(k, s).start()

    def gram_f(k):
        for s in range(1, ratio):
            ge_in(k, s).wait()
        for m in range(pairs):
            for i in range(nrow):
                for s in range(ratio):
                    at = pl.ds(i * strip + s * thin, thin)
                    gram[k, m, at] = decode(gq.at[k, s, i, m], thin)

    def keep(k, m, x):
        fact[k, m, 0], fact[k, m, 1] = halves(x)

    def kept(k, m):
        return fact[k, m, 0], fact[k, m, 1]

    def make_c():
        keep(0, 0, -fix * gram[0, 0])
        keep(0, 2, -fix * gram[0, 2])
        keep(0, 1, dot2(kept(0, 0), kept(0, 2), NN) - fix * gram[0, 1])

    def make_d():
        keep(1, 0, -fix * gram[1, 0])
        keep(1, 1, dot2(kept(1, 0), kept(0, 2), NN) - fix * gram[1, 1])
        last = (
            gram[1, 2]
            + dot2(kept(0, 0), halves(gram[1, 1]), TN)
            + dot2(kept(1, 0), halves(gram[0, 1]), TN)
        )
        keep(1, 2, -fix * last)

    def both(x):
        return x[0], x[1]

    def full(x):
        return x[0].astype(jnp.float32) + x[1].astype(jnp.float32)

    def make_z():
        zt[0, 0], zt[0, 1] = halves(
            vtt[0].astype(jnp.float32)
            + dot4(kept(0, 0), vtt[1], NN) + dot4(kept(0, 1), vtt[2], NN)
        )
        zt[1, 0], zt[1, 1] = halves(vtt[1].astype(jnp.float32) + dot4(kept(0, 2), vtt[2], NN))

    def minus(terms):
        out_ref[...] = out_ref[...] - half * terms


    for t in range(ticks):
        if t == 1:
            @pl.when(stays)
            def _():
                vt_in.start()

            @pl.when(jnp.logical_not(stays))
            def _():
                vt_move.start()
        for i in range(1, links):
            v_out(t, i).start()
        for k in range(1, ratio):
            v_side(t, 0, k).start()

    a_in.wait()
    ab[0], ab[1] = halves(a_ref[...])

    partial(0)
    vt_spread()
    partial(1)
    collect(0)
    vt_close()
    gram_a(0)
    collect(1)
    gram_a(1)
    gram_b(0)
    gram_b(1)
    partial(2)
    relay(0)
    open_cols(0)
    gram_d(0)
    collect(2)
    gram_d(1)
    relay(1)
    open_cols(1)
    gram_e(0)
    open_rows(0)
    gram_e(1)
    gram_f(0)
    make_c()
    make_z()
    out_ref[...] = a_ref[...]
    minus(dot2(both(wr.at[0]), both(zt.at[0]), NN))
    relay(2)
    open_cols(2)
    open_rows(1)
    minus(dot2(both(wr.at[1]), both(zt.at[1]), NN))
    one = full(wct.at[1]) + dot2(kept(0, 0), both(wct.at[0]), TN)
    two = (
        full(wct.at[2]) + dot2(kept(0, 1), both(wct.at[0]), TN)
        + dot2(kept(0, 2), both(wct.at[1]), TN)
    )
    part[1] = one
    part[2] = two
    gram_f(1)
    make_d()
    zero = full(wct.at[0]) + dot4(kept(1, 0), vtt[1], NN) + dot4(kept(1, 1), vtt[2], NN)
    minus(dot3(vr[0], halves(zero), NN))
    one = part[1] + dot4(kept(1, 0), vtt[0], TN) + dot4(kept(1, 2), vtt[2], NN)
    minus(dot3(vr[1], halves(one), NN))
    two = part[2] + dot4(kept(1, 1), vtt[0], TN) + dot4(kept(1, 2), vtt[1], TN)
    minus(dot3(vr[2], halves(two), NN))
    open_rows(2)
    minus(dot4(both(wr.at[2]), vtt[2], NN))
    mine = rows(c)
    for t in range(ticks):
        total = wr[t, 0, mine].astype(jnp.float32) + wr[t, 1, mine].astype(jnp.float32)
        for m, (u, later) in enumerate(chosen):
            if later == t:
                total = total + dot2((wr[u, 0, mine], wr[u, 1, mine]), kept(0, m), NN)
                total = total + dot3(vr[u, mine], kept(1, m), NN)
        w_ref[t] = total

    for t in range(ticks):
        for i in range(1, links):
            v_out(t, i).wait_send()
            wr_out(t, i).wait_send()
        for k in range(1, ratio):
            for i in range(links):
                v_side(t, i, k).wait_send()
            wx_out(t, k).wait_send()
        for i in range(1, nrow):
            vt_out(t, i).wait_send()
            rs_out(t, i).wait_send()
            wc_out(t, i).wait_send()

    for k in range(2):
        for s in range(1, ratio):
            ga_out(k, s).wait_send()
            ge_out(k, s).wait_send()
        for s in range(1, links):
            gb_out(k, s).wait_send()
        for i in range(1, nrow):
            gd_out(k, i).wait_send()


def on_device(trailing, v_panels):
    nrow = lax.axis_size("row")
    ncol = lax.axis_size("col")
    rows_tile, cols_tile = trailing.shape
    ticks, piece, depth = v_panels.shape
    ratio = rows_tile // cols_tile
    links = ncol // ratio
    scaling = 1.0 / math.sqrt(rows_tile * nrow)
    pairs = ticks * (ticks - 1) // 2
    strip = depth // nrow
    thin = strip // ratio
    dma = pltpu.SemaphoreType.DMA
    vmem = pl.BlockSpec(memory_space=pltpu.VMEM)
    f32, bf16 = jnp.float32, jnp.bfloat16
    return pl.pallas_call(
        functools.partial(kernel, nrow, ncol, ratio, scaling),
        out_shape=(
            jax.ShapeDtypeStruct(trailing.shape, f32),
            jax.ShapeDtypeStruct(v_panels.shape, f32),
        ),
        in_specs=[pl.BlockSpec(memory_space=pltpu.MemorySpace.HBM)] * 2,
        out_specs=(vmem, vmem),
        scratch_shapes=[
            pltpu.VMEM((rows_tile, cols_tile), f32),
            pltpu.VMEM((2, rows_tile, cols_tile), bf16),
            pltpu.VMEM((ticks, rows_tile, depth), bf16),
            pltpu.VMEM((ticks, cols_tile, depth), bf16),
            pltpu.VMEM((ticks, depth, cols_tile), bf16),
            pltpu.VMEM((ticks, depth, cols_tile), f32),
            pltpu.VMEM((ticks, nrow, strip + TILE, cols_tile), bf16),
            pltpu.VMEM((ticks, nrow, strip + TILE, cols_tile), bf16),
            pltpu.VMEM((ticks, 2, strip, cols_tile), bf16),
            pltpu.VMEM((ticks, nrow, strip + TILE, cols_tile), bf16),
            pltpu.VMEM((ticks, ratio, nrow, strip + TILE, cols_tile), bf16),
            pltpu.VMEM((ticks, 2, depth, cols_tile), bf16),
            pltpu.VMEM((ticks, 2, rows_tile, depth), bf16),
            pltpu.VMEM((ticks - 1, 2, depth, cols_tile), bf16),
            pltpu.VMEM((2, pairs, strip, depth), f32),
            pltpu.VMEM((2, ratio, pairs, thin, depth), f32),
            pltpu.VMEM((2, pairs, thin + TILE, depth), bf16),
            pltpu.VMEM((2, links, pairs, thin + TILE, depth), bf16),
            pltpu.VMEM((2, ratio, nrow, pairs, thin + TILE, depth), bf16),
            pltpu.VMEM((2, pairs, depth, depth), f32),
            pltpu.VMEM((2, pairs, 2, depth, depth), bf16),
            dma((ticks, links)),
            dma((ticks, ncol)),
            dma,
            dma,
            dma((ticks, links, ratio)),
            dma((ticks, nrow)),
            dma((ticks, nrow)),
            dma((ticks, nrow)),
            dma((ticks, nrow)),
            dma((ticks, nrow)),
            dma((ticks, nrow)),
            dma((ticks, links)),
            dma((ticks, nrow)),
            dma((ticks, ratio)),
            dma((ticks, ratio)),
            dma((ticks,)),
            dma((2,)),
            dma((2, ratio)), dma((2, ratio)),
            dma((2, links)), dma((2, links)),
            dma((2, nrow)), dma((2, nrow)),
            dma((2, ratio)), dma((2, ratio)),
        ],
        compiler_params=pltpu.CompilerParams(
            collective_id=0, has_side_effects=True, vmem_limit_bytes=48 * 1024 * 1024
        ),
    )(trailing, v_panels)


def solution(mesh):
    in_specs = (P("row", "col"), P(None, ("row", "col"), None))
    out_specs = (P("row", "col"), P(None, ("row", "col"), None))
    return jax.shard_map(
        on_device, mesh=mesh, in_specs=in_specs, out_specs=out_specs, check_vma=False
    )
```

```python
import functools
import math

import jax
import jax.numpy as jnp
from jax import lax
from jax.experimental import pallas as pl
from jax.experimental.pallas import tpu as pltpu
from jax.sharding import PartitionSpec as P

MESH = pl.DeviceIdType.MESH
NT = (((1,), (1,)), ((), ()))
NN = (((1,), (0,)), ((), ()))
TN = (((0,), (0,)), ((), ()))
SPAN = 124.0
TINY = 1e-30
TILE = 8


def dot(a, b, dims):
    return lax.dot_general(a, b, dims, preferred_element_type=jnp.float32)


def halves(x):
    high = x.astype(jnp.bfloat16)
    return high, (x - high.astype(jnp.float32)).astype(jnp.bfloat16)


def dot2(a, b, dims):
    return dot(a[0], b[0], dims) + (dot(a[0], b[1], dims) + dot(a[1], b[0], dims))


def dot3(a, b, dims):
    return dot(a, b[0], dims) + dot(a, b[1], dims)


def dot4(a, b, dims):
    return dot(a[0], b, dims) + dot(a[1], b, dims)


def encode(ref, x):
    rows = x.shape[0]
    peak = jnp.maximum(jnp.max(jnp.abs(x), axis=0, keepdims=True), TINY).astype(jnp.bfloat16)
    ref[pl.ds(0, rows)] = jnp.exp2(x * (SPAN / peak.astype(jnp.float32))).astype(jnp.bfloat16)
    ref[pl.ds(ref.shape[0] - TILE, TILE)] = jnp.broadcast_to(peak, (TILE, x.shape[1]))


def decode(ref, rows):
    peak = ref[pl.ds(ref.shape[0] - TILE, TILE)].astype(jnp.float32)[:1]
    return jnp.log2(ref[pl.ds(0, rows)].astype(jnp.float32)) * (peak * (1.0 / SPAN))


def kernel(
    nrow, ncol, ratio, scaling,
    a_hbm, v_ref, out_ref, w_ref,
    a_ref, ab, vo, vr, vt, vtt, part, sent, got, own, wcc, wrc, wct, wr, zt, gp, ga, gs, gc, gq, gram, fact,
    v_send, v_recv, vt_send, vt_recv, vx_send, vo_send, vx_recv, vs_send, vs_recv, vl_sem,
    rs_send, rs_recv, wc_send, wc_recv, wr_send, wr_recv, wx_send, wx_recv, local_sem, in_sem,
    ga_send, ga_recv, gb_send, gb_recv, gd_send, gd_recv, ge_send, ge_recv,
):
    ticks, piece, depth = v_ref.shape
    rows_tile, cols_tile = a_hbm.shape
    links = ncol // ratio
    chosen = [(u, t) for t in range(ticks) for u in range(t)]
    pairs = len(chosen)
    r = lax.axis_index("row")
    c = lax.axis_index("col")
    q = c // ratio
    j = c % ratio
    half = 0.5 * scaling
    fix = scaling * half
    strip = depth // nrow
    thin = strip // ratio

    def rows(at):
        return pl.ds(pl.multiple_of(at * piece, piece), piece)

    def strips(at):
        return pl.ds(pl.multiple_of(at * strip, strip), strip)

    def thins(at):
        return pl.ds(pl.multiple_of(at * thin, thin), thin)

    def remote(src, dst, send, recv, row, col):
        return pltpu.make_async_remote_copy(
            src_ref=src, dst_ref=dst, send_sem=send, recv_sem=recv,
            device_id=(row, col), device_id_type=MESH,
        )

    from_row, from_col = c // ratio, j * nrow + r
    to_row, to_col = c % nrow, r * ratio + c // nrow
    stays = jnp.logical_and(to_row == r, to_col == c)

    a_in = pltpu.make_async_copy(a_hbm, a_ref, in_sem.at[0])
    v_own = pltpu.make_async_copy(v_ref, vr.at[:, rows(c)], in_sem.at[1])
    v_src = pltpu.make_async_copy(v_ref, vo, in_sem.at[2])
    v_src.start()
    v_own.start()
    a_in.start()
    barrier = pltpu.get_barrier_semaphore()

    def greet(row, col):
        pl.semaphore_signal(barrier, inc=1, device_id=(row, col), device_id_type=MESH)

    for i in range(1, nrow):
        greet((r + i) % nrow, c)
    for k in range(1, ratio):
        greet(r, q * ratio + (j + k) % ratio)
    for i in range(1, links):
        greet(r, ((q + i) % links) * ratio + j)

    @pl.when(jnp.logical_not(stays))
    def _():
        greet(from_row, from_col)
        greet(to_row, to_col)

    v_src.wait()
    v_own.wait()
    pl.semaphore_wait(barrier, nrow + ratio + links - 3 + jnp.where(stays, 0, 2))

    def start(copy):
        copy.start()

    def wait_send(copy):
        copy.wait_send()

    def v_out(t, i):
        return remote(
            vo.at[t], vr.at[t, rows(c)], v_send.at[t, i], v_recv.at[t, c],
            r, ((q + i) % links) * ratio + j,
        )

    def v_side(t, i, k):
        at = ((q + i) % links) * ratio + j
        spot = vr.at[t, rows(at)]
        return remote(
            spot if i else vo.at[t], spot, vx_send.at[t, i, k - 1], v_recv.at[t, at],
            r, q * ratio + (j + k) % ratio,
        )

    def v_in(t, col):
        spot = vr.at[t, rows(col)]
        return pltpu.make_async_copy(spot, spot, v_recv.at[t, col])

    def vt_move(t):
        return remote(
            vo.at[t], vt.at[t, rows(to_row)], vt_send.at[t], vt_recv.at[t], to_row, to_col
        )

    def vt_in(t):
        return pltpu.make_async_copy(vo.at[t], vt.at[t, rows(r)], vt_recv.at[t])

    def vt_start(t):
        @pl.when(stays)
        def _():
            vt_in(t).start()

        @pl.when(jnp.logical_not(stays))
        def _():
            vt_move(t).start()

    def vt_out(t, i):
        peer = (r + i) % nrow
        spot = vt.at[t, rows(r)]
        return remote(spot, spot, vo_send.at[t, i], vx_recv.at[t, r], peer, c)

    def vt_got(t, peer):
        spot = vt.at[t, rows(peer)]
        return pltpu.make_async_copy(spot, spot, vx_recv.at[t, peer])

    source = q == r
    aside = jnp.logical_not(source)

    def seats(at):
        return pl.ds(pl.multiple_of(at * cols_tile, cols_tile), cols_tile)

    def vs_out(t, k):
        return remote(
            vt.at[t], vr.at[t, seats(j)], vs_send.at[t, k], vs_recv.at[t, j],
            r, q * ratio + (j + k) % ratio,
        )

    def vs_in(t, k):
        at = (j + k) % ratio
        spot = vr.at[t, seats(at)]
        return pltpu.make_async_copy(spot, spot, vs_recv.at[t, at])

    def vs_keep(t):
        return pltpu.make_async_copy(vt.at[t], vr.at[t, seats(j)], vl_sem.at[t])

    def v_each(t, act):
        for i in range(1, links):
            if t == 0:
                act(v_out(t, i))
            else:
                @pl.when((q + i) % links != r)
                def _():
                    act(v_out(t, i))
        if t == 0:
            for k in range(1, ratio):
                act(v_side(t, 0, k))
        else:
            @pl.when(aside)
            def _():
                for k in range(1, ratio):
                    act(v_side(t, 0, k))

    def v_direct(t):
        for i in range(1, links):
            v_in(t, ((q + i) % links) * ratio + j).wait()
            for k in range(1, ratio):
                v_side(t, i, k).start()
        for i in range(links):
            for k in range(1, ratio):
                v_in(t, ((q + i) % links) * ratio + (j + k) % ratio).wait()

    closed, gathered = set(), set()

    def v_gather(t):
        if t == 0:
            v_direct(t)
            return

        gathered.add(t)

        @pl.when(aside)
        def _():
            v_direct(t)

        @pl.when(source)
        def _():
            if t not in closed:
                vt_arrive(t)
            vs_keep(t).start()
            for k in range(1, ratio):
                vs_out(t, k).start()
            for k in range(1, ratio):
                vs_in(t, k).wait()
            vs_keep(t).wait()

    def vt_spread(t):
        @pl.when(stays)
        def _():
            vt_in(t).wait()

        @pl.when(jnp.logical_not(stays))
        def _():
            vt_move(t).wait()

        for i in range(1, nrow):
            vt_out(t, i).start()

    def vt_arrive(t):
        for i in range(1, nrow):
            vt_got(t, (r + i) % nrow).wait()

    def vt_close(t):
        if t in gathered:
            @pl.when(aside)
            def _():
                vt_arrive(t)
        else:
            vt_arrive(t)
            closed.add(t)
        vtt[t] = vt[t].astype(jnp.float32).T.astype(jnp.bfloat16)

    def rs_out(t, i):
        peer = (r + i) % nrow
        return remote(
            sent.at[t, peer], got.at[t, r], rs_send.at[t, i], rs_recv.at[t, r], peer, c
        )

    def rs_in(t, peer):
        return pltpu.make_async_copy(sent.at[t, peer], got.at[t, peer], rs_recv.at[t, peer])

    def wc_out(t, i):
        spot = wcc.at[t, r]
        return remote(spot, spot, wc_send.at[t, i], wc_recv.at[t, r], (r + i) % nrow, c)

    def wc_in(t, peer):
        spot = wcc.at[t, peer]
        return pltpu.make_async_copy(spot, spot, wc_recv.at[t, peer])

    def wr_out(t, i):
        return remote(
            wcc.at[t, r], wrc.at[t, j, r], wr_send.at[t, i], wr_recv.at[t, r],
            q, ((q + i) % links) * ratio + j,
        )

    def wr_in(t, peer):
        spot = wrc.at[t, j, peer]
        return pltpu.make_async_copy(spot, spot, wr_recv.at[t, peer])

    def wr_keep(t):
        return pltpu.make_async_copy(wcc.at[t], wrc.at[t, j], local_sem.at[t])

    def wx_out(t, k):
        spot = wrc.at[t, j]
        return remote(
            spot, spot, wx_send.at[t, k], wx_recv.at[t, j], r, q * ratio + (j + k) % ratio
        )

    def wx_in(t, k):
        at = (j + k) % ratio
        spot = wrc.at[t, at]
        return pltpu.make_async_copy(spot, spot, wx_recv.at[t, at])

    def partial(t):
        v_gather(t)
        part[t] = dot(vr[t], ab[0], TN) + dot(vr[t], ab[1], TN)
        for i in range(1, nrow):
            peer = (r + i) % nrow
            encode(sent.at[t, peer], part[t, strips(peer)])
            rs_out(t, i).start()

    def collect(t):
        total = part[t, strips(r)]
        for i in range(1, nrow):
            peer = (r + i) % nrow
            rs_in(t, peer).wait()
            total = total + decode(got.at[t, peer], strip)
        total = total * scaling
        encode(wcc.at[t, r], total)
        own[t, 0], own[t, 1] = halves(total)

    def spread(t):
        for i in range(1, nrow):
            wc_out(t, i).start()
        for i in range(1, links):
            wr_out(t, i).start()

    def relay(t):
        for i in range(1, nrow):
            wc_in(t, (r + i) % nrow).wait()

        @pl.when(source)
        def _():
            wr_keep(t).start()
            wr_keep(t).wait()

        @pl.when(jnp.logical_not(source))
        def _():
            for i in range(nrow):
                wr_in(t, (r + i) % nrow).wait()

        for k in range(1, ratio):
            wx_out(t, k).start()

    def open_cols(t):
        for k in range(nrow):
            at = pl.ds(k * strip, strip)
            wct[t, 0, at], wct[t, 1, at] = halves(decode(wcc.at[t, k], strip))

    def open_rows(t):
        for k in range(1, ratio):
            wx_in(t, k).wait()
        for s in range(ratio):
            x = jnp.concatenate([decode(wrc.at[t, s, k], strip) for k in range(nrow)], axis=0)
            at = pl.ds(s * cols_tile, cols_tile)
            wr[t, 0, at], wr[t, 1, at] = halves(x.T)

    def ga_out(k, s):
        to = (j + s) % ratio
        return remote(
            gp.at[k, :, thins(to)], ga.at[k, j], ga_send.at[k, s], ga_recv.at[k, j],
            r, q * ratio + to,
        )

    def ga_in(k, s):
        at = (j + s) % ratio
        return pltpu.make_async_copy(ga.at[k, at], ga.at[k, at], ga_recv.at[k, at])

    def gb_out(k, s):
        return remote(
            gs.at[k], gc.at[k, q], gb_send.at[k, s], gb_recv.at[k, q],
            r, ((q + s) % links) * ratio + j,
        )

    def gb_in(k, s):
        at = (q + s) % links
        return pltpu.make_async_copy(gc.at[k, at], gc.at[k, at], gb_recv.at[k, at])

    def gd_out(k, i):
        spot = gq.at[k, j, r]
        return remote(spot, spot, gd_send.at[k, i], gd_recv.at[k, r], (r + i) % nrow, c)

    def gd_in(k, i):
        at = (r + i) % nrow
        spot = gq.at[k, j, at]
        return pltpu.make_async_copy(spot, spot, gd_recv.at[k, at])

    def ge_out(k, s):
        spot = gq.at[k, j]
        return remote(
            spot, spot, ge_send.at[k, s], ge_recv.at[k, j], r, q * ratio + (j + s) % ratio
        )

    def ge_in(k, s):
        at = (j + s) % ratio
        spot = gq.at[k, at]
        return pltpu.make_async_copy(spot, spot, ge_recv.at[k, at])

    def gram_a(k):
        for m, (u, t) in enumerate(chosen):
            gp[k, m] = dot4(own.at[u], vt[t], NN) if k else dot(vtt[u, strips(r)], vt[t], NN)
        for s in range(1, ratio):
            ga_out(k, s).start()

    def gram_b(k):
        for s in range(1, ratio):
            ga_in(k, s).wait()
        for m in range(pairs):
            total = gp[k, m, thins(j)]
            for s in range(1, ratio):
                total = total + ga[k, (j + s) % ratio, m]
            gp[k, m, thins(j)] = total
            encode(gs.at[k, m], total)
        for s in range(1, links):
            gb_out(k, s).start()

    def gram_d(k):
        for s in range(1, links):
            gb_in(k, s).wait()
        for m in range(pairs):
            total = gp[k, m, thins(j)]
            for s in range(1, links):
                total = total + decode(gc.at[k, (q + s) % links, m], thin)
            encode(gq.at[k, j, r, m], total)
        for i in range(1, nrow):
            gd_out(k, i).start()

    def gram_e(k):
        for i in range(1, nrow):
            gd_in(k, i).wait()
        for s in range(1, ratio):
            ge_out(k, s).start()

    def gram_f(k):
        for s in range(1, ratio):
            ge_in(k, s).wait()
        for m in range(pairs):
            for i in range(nrow):
                for s in range(ratio):
                    at = pl.ds(i * strip + s * thin, thin)
                    gram[k, m, at] = decode(gq.at[k, s, i, m], thin)

    def keep(k, m, x):
        fact[k, m, 0], fact[k, m, 1] = halves(x)

    def kept(k, m):
        return fact[k, m, 0], fact[k, m, 1]

    def make_c():
        keep(0, 0, -fix * gram[0, 0])
        keep(0, 2, -fix * gram[0, 2])
        keep(0, 1, dot2(kept(0, 0), kept(0, 2), NN) - fix * gram[0, 1])

    def make_d():
        keep(1, 0, -fix * gram[1, 0])
        keep(1, 1, dot2(kept(1, 0), kept(0, 2), NN) - fix * gram[1, 1])
        last = (
            gram[1, 2]
            + dot2(kept(0, 0), halves(gram[1, 1]), TN)
            + dot2(kept(1, 0), halves(gram[0, 1]), TN)
        )
        keep(1, 2, -fix * last)

    def both(x):
        return x[0], x[1]

    def full(x):
        return x[0].astype(jnp.float32) + x[1].astype(jnp.float32)

    def make_z():
        zt[0, 0], zt[0, 1] = halves(
            vtt[0].astype(jnp.float32)
            + dot4(kept(0, 0), vtt[1], NN) + dot4(kept(0, 1), vtt[2], NN)
        )
        zt[1, 0], zt[1, 1] = halves(vtt[1].astype(jnp.float32) + dot4(kept(0, 2), vtt[2], NN))

    def minus(terms):
        out_ref[...] = out_ref[...] - half * terms


    vt_start(1)
    a_in.wait()
    ab[0], ab[1] = halves(a_ref[...])
    out_ref[...] = a_ref[...]
    vt_start(2)
    v_each(1, start)
    vt_start(0)
    vt_spread(1)
    vt_spread(2)
    v_each(0, start)
    vt_spread(0)
    partial(1)
    v_each(2, start)
    partial(0)
    collect(1)
    spread(1)
    vt_close(2)
    vt_close(1)
    collect(0)
    vt_close(0)
    gram_a(0)
    spread(0)
    partial(2)
    gram_b(0)
    gram_a(1)
    gram_b(1)
    relay(1)
    gram_d(0)
    collect(2)
    relay(0)
    spread(2)
    open_cols(0)
    open_rows(1)
    gram_d(1)
    open_rows(0)
    open_cols(1)
    gram_e(0)
    gram_f(0)
    make_c()
    relay(2)
    open_cols(2)
    make_z()
    gram_e(1)
    part[1] = full(wct.at[1]) + dot2(kept(0, 0), both(wct.at[0]), TN)
    part[2] = (
        full(wct.at[2]) + dot2(kept(0, 1), both(wct.at[0]), TN)
        + dot2(kept(0, 2), both(wct.at[1]), TN)
    )
    open_rows(2)
    gram_f(1)
    make_d()
    zero = full(wct.at[0]) + dot4(kept(1, 0), vtt[1], NN) + dot4(kept(1, 1), vtt[2], NN)
    minus(dot3(vr[0], halves(zero), NN))
    one = part[1] + dot4(kept(1, 0), vtt[0], TN) + dot4(kept(1, 2), vtt[2], NN)
    minus(dot3(vr[1], halves(one), NN))
    two = part[2] + dot4(kept(1, 1), vtt[0], TN) + dot4(kept(1, 2), vtt[1], TN)
    minus(dot3(vr[2], halves(two), NN))
    minus(dot4(both(wr.at[2]), vtt[2], NN))
    mine = rows(c)
    for t in range(ticks):
        total = wr[t, 0, mine].astype(jnp.float32) + wr[t, 1, mine].astype(jnp.float32)
        for m, (u, later) in enumerate(chosen):
            if later == t:
                total = total + dot2((wr[u, 0, mine], wr[u, 1, mine]), kept(0, m), NN)
                total = total + dot3(vr[u, mine], kept(1, m), NN)
        w_ref[t] = total
    minus(dot2(both(wr.at[1]), both(zt.at[1]), NN))
    minus(dot2(both(wr.at[0]), both(zt.at[0]), NN))

    for t in range(ticks):
        v_each(t, wait_send)
        for i in range(1, links):
            wr_out(t, i).wait_send()
        for k in range(1, ratio):
            if t == 0:
                for i in range(1, links):
                    v_side(t, i, k).wait_send()
            else:
                @pl.when(aside)
                def _():
                    for i in range(1, links):
                        v_side(t, i, k).wait_send()

                @pl.when(source)
                def _():
                    vs_out(t, k).wait_send()
            wx_out(t, k).wait_send()
        for i in range(1, nrow):
            vt_out(t, i).wait_send()
            rs_out(t, i).wait_send()
            wc_out(t, i).wait_send()

    for k in range(2):
        for s in range(1, ratio):
            ga_out(k, s).wait_send()
            ge_out(k, s).wait_send()
        for s in range(1, links):
            gb_out(k, s).wait_send()
        for i in range(1, nrow):
            gd_out(k, i).wait_send()


def on_device(trailing, v_panels):
    nrow = lax.axis_size("row")
    ncol = lax.axis_size("col")
    rows_tile, cols_tile = trailing.shape
    ticks, piece, depth = v_panels.shape
    ratio = rows_tile // cols_tile
    links = ncol // ratio
    scaling = 1.0 / math.sqrt(rows_tile * nrow)
    pairs = ticks * (ticks - 1) // 2
    strip = depth // nrow
    thin = strip // ratio
    dma = pltpu.SemaphoreType.DMA
    vmem = pl.BlockSpec(memory_space=pltpu.VMEM)
    f32, bf16 = jnp.float32, jnp.bfloat16
    return pl.pallas_call(
        functools.partial(kernel, nrow, ncol, ratio, scaling),
        out_shape=(
            jax.ShapeDtypeStruct(trailing.shape, f32),
            jax.ShapeDtypeStruct(v_panels.shape, f32),
        ),
        in_specs=[pl.BlockSpec(memory_space=pltpu.MemorySpace.HBM)] * 2,
        out_specs=(vmem, vmem),
        scratch_shapes=[
            pltpu.VMEM((rows_tile, cols_tile), f32),
            pltpu.VMEM((2, rows_tile, cols_tile), bf16),
            pltpu.VMEM((ticks, piece, depth), bf16),
            pltpu.VMEM((ticks, rows_tile, depth), bf16),
            pltpu.VMEM((ticks, cols_tile, depth), bf16),
            pltpu.VMEM((ticks, depth, cols_tile), bf16),
            pltpu.VMEM((ticks, depth, cols_tile), f32),
            pltpu.VMEM((ticks, nrow, strip + TILE, cols_tile), bf16),
            pltpu.VMEM((ticks, nrow, strip + TILE, cols_tile), bf16),
            pltpu.VMEM((ticks, 2, strip, cols_tile), bf16),
            pltpu.VMEM((ticks, nrow, strip + TILE, cols_tile), bf16),
            pltpu.VMEM((ticks, ratio, nrow, strip + TILE, cols_tile), bf16),
            pltpu.VMEM((ticks, 2, depth, cols_tile), bf16),
            pltpu.VMEM((ticks, 2, rows_tile, depth), bf16),
            pltpu.VMEM((ticks - 1, 2, depth, cols_tile), bf16),
            pltpu.VMEM((2, pairs, strip, depth), f32),
            pltpu.VMEM((2, ratio, pairs, thin, depth), f32),
            pltpu.VMEM((2, pairs, thin + TILE, depth), bf16),
            pltpu.VMEM((2, links, pairs, thin + TILE, depth), bf16),
            pltpu.VMEM((2, ratio, nrow, pairs, thin + TILE, depth), bf16),
            pltpu.VMEM((2, pairs, depth, depth), f32),
            pltpu.VMEM((2, pairs, 2, depth, depth), bf16),
            dma((ticks, links)),
            dma((ticks, ncol)),
            dma((ticks,)),
            dma((ticks,)),
            dma((ticks, links, ratio)),
            dma((ticks, nrow)),
            dma((ticks, nrow)),
            dma((ticks, ratio)),
            dma((ticks, ratio)),
            dma((ticks,)),
            dma((ticks, nrow)),
            dma((ticks, nrow)),
            dma((ticks, nrow)),
            dma((ticks, nrow)),
            dma((ticks, links)),
            dma((ticks, nrow)),
            dma((ticks, ratio)),
            dma((ticks, ratio)),
            dma((ticks,)),
            dma((3,)),
            dma((2, ratio)), dma((2, ratio)),
            dma((2, links)), dma((2, links)),
            dma((2, nrow)), dma((2, nrow)),
            dma((2, ratio)), dma((2, ratio)),
        ],
        compiler_params=pltpu.CompilerParams(
            collective_id=0, has_side_effects=True, vmem_limit_bytes=48 * 1024 * 1024
        ),
    )(trailing, v_panels)


def solution(mesh):
    in_specs = (P("row", "col"), P(None, ("row", "col"), None))
    out_specs = (P("row", "col"), P(None, ("row", "col"), None))
    return jax.shard_map(
        on_device, mesh=mesh, in_specs=in_specs, out_specs=out_specs, check_vma=False
    )
```

```python
import functools
import math

import jax
import jax.numpy as jnp
from jax import lax
from jax.experimental import pallas as pl
from jax.experimental.pallas import tpu as pltpu
from jax.sharding import PartitionSpec as P

MESH = pl.DeviceIdType.MESH
NT = (((1,), (1,)), ((), ()))
NN = (((1,), (0,)), ((), ()))
TN = (((0,), (0,)), ((), ()))
SPAN = 124.0
TINY = 1e-30
TILE = 8


def dot(a, b, dims):
    return lax.dot_general(a, b, dims, preferred_element_type=jnp.float32)


def halves(x):
    high = x.astype(jnp.bfloat16)
    return high, (x - high.astype(jnp.float32)).astype(jnp.bfloat16)


def dot2(a, b, dims):
    return dot(a[0], b[0], dims) + (dot(a[0], b[1], dims) + dot(a[1], b[0], dims))


def dot3(a, b, dims):
    return dot(a, b[0], dims) + dot(a, b[1], dims)


def dot4(a, b, dims):
    return dot(a[0], b, dims) + dot(a[1], b, dims)


def encode(ref, x):
    rows = x.shape[0]
    peak = jnp.maximum(jnp.max(jnp.abs(x), axis=0, keepdims=True), TINY).astype(jnp.bfloat16)
    ref[pl.ds(0, rows)] = jnp.exp2(x * (SPAN / peak.astype(jnp.float32))).astype(jnp.bfloat16)
    ref[pl.ds(ref.shape[0] - TILE, TILE)] = jnp.broadcast_to(peak, (TILE, x.shape[1]))


def encode_all(ref, parts):
    rows = parts[0].shape[0]
    peak = jnp.max(jnp.abs(parts[0]), axis=0, keepdims=True)
    for x in parts[1:]:
        peak = jnp.maximum(peak, jnp.max(jnp.abs(x), axis=0, keepdims=True))
    peak = jnp.maximum(peak, TINY).astype(jnp.bfloat16)
    scale = SPAN / peak.astype(jnp.float32)
    for i, x in enumerate(parts):
        ref[pl.ds(i * rows, rows)] = jnp.exp2(x * scale).astype(jnp.bfloat16)
    ref[pl.ds(ref.shape[0] - TILE, TILE)] = jnp.broadcast_to(peak, (TILE, peak.shape[1]))


def decode(ref, rows, at=0):
    peak = ref[pl.ds(ref.shape[0] - TILE, TILE)].astype(jnp.float32)[:1]
    return jnp.log2(ref[pl.ds(at, rows)].astype(jnp.float32)) * (peak * (1.0 / SPAN))


def kernel(
    nrow, ncol, ratio, scaling,
    a_hbm, v_ref, out_ref, w_ref,
    a_ref, ab, vo, vr, vt, vtt, part, sent, got, own, wcc, wrc, wct, wr, zt, gp, gt, ga, gs, gc, gq, gram, fact,
    v_send, v_recv, vt_send, vt_recv, vx_send, vo_send, vx_recv, vs_send, vs_recv, vl_sem,
    rs_send, rs_recv, wc_send, wc_recv, wr_send, wr_recv, wx_send, wx_recv, local_sem, in_sem,
    ga_send, ga_recv, gb_send, gb_recv, gd_send, gd_recv, ge_send, ge_recv,
):
    ticks, piece, depth = v_ref.shape
    rows_tile, cols_tile = a_hbm.shape
    links = ncol // ratio
    chosen = [(u, t) for t in range(ticks) for u in range(t)]
    pairs = len(chosen)
    r = lax.axis_index("row")
    c = lax.axis_index("col")
    q = c // ratio
    j = c % ratio
    half = 0.5 * scaling
    fix = scaling * half
    strip = depth // nrow
    thin = strip // ratio
    steps = gs.shape[1]

    def rows(at):
        return pl.ds(pl.multiple_of(at * piece, piece), piece)

    def strips(at):
        return pl.ds(pl.multiple_of(at * strip, strip), strip)

    def thins(at):
        return pl.ds(pl.multiple_of(at * thin, thin), thin)

    def remote(src, dst, send, recv, row, col):
        return pltpu.make_async_remote_copy(
            src_ref=src, dst_ref=dst, send_sem=send, recv_sem=recv,
            device_id=(row, col), device_id_type=MESH,
        )

    from_row, from_col = c // ratio, j * nrow + r
    to_row, to_col = c % nrow, r * ratio + c // nrow
    stays = jnp.logical_and(to_row == r, to_col == c)

    a_in = pltpu.make_async_copy(a_hbm, a_ref, in_sem.at[0])
    v_own = pltpu.make_async_copy(v_ref, vr.at[:, rows(c)], in_sem.at[1])
    v_src = pltpu.make_async_copy(v_ref, vo, in_sem.at[2])
    v_src.start()
    v_own.start()
    a_in.start()
    barrier = pltpu.get_barrier_semaphore()

    def greet(row, col):
        pl.semaphore_signal(barrier, inc=1, device_id=(row, col), device_id_type=MESH)

    for i in range(1, nrow):
        greet((r + i) % nrow, c)
    for k in range(1, ratio):
        greet(r, q * ratio + (j + k) % ratio)
    for i in range(1, links):
        greet(r, ((q + i) % links) * ratio + j)

    @pl.when(jnp.logical_not(stays))
    def _():
        greet(from_row, from_col)
        greet(to_row, to_col)

    v_src.wait()
    v_own.wait()
    pl.semaphore_wait(barrier, nrow + ratio + links - 3 + jnp.where(stays, 0, 2))

    def start(copy):
        copy.start()

    def wait_send(copy):
        copy.wait_send()

    def v_out(t, i):
        return remote(
            vo.at[t], vr.at[t, rows(c)], v_send.at[t, i], v_recv.at[t, c],
            r, ((q + i) % links) * ratio + j,
        )

    def v_side(t, i, k):
        at = ((q + i) % links) * ratio + j
        spot = vr.at[t, rows(at)]
        return remote(
            spot if i else vo.at[t], spot, vx_send.at[t, i, k - 1], v_recv.at[t, at],
            r, q * ratio + (j + k) % ratio,
        )

    def v_in(t, col):
        spot = vr.at[t, rows(col)]
        return pltpu.make_async_copy(spot, spot, v_recv.at[t, col])

    def vt_move(t):
        return remote(
            vo.at[t], vt.at[t, rows(to_row)], vt_send.at[t], vt_recv.at[t], to_row, to_col
        )

    def vt_in(t):
        return pltpu.make_async_copy(vo.at[t], vt.at[t, rows(r)], vt_recv.at[t])

    def vt_start(t):
        @pl.when(stays)
        def _():
            vt_in(t).start()

        @pl.when(jnp.logical_not(stays))
        def _():
            vt_move(t).start()

    def vt_out(t, i):
        peer = (r + i) % nrow
        spot = vt.at[t, rows(r)]
        return remote(spot, spot, vo_send.at[t, i], vx_recv.at[t, r], peer, c)

    def vt_got(t, peer):
        spot = vt.at[t, rows(peer)]
        return pltpu.make_async_copy(spot, spot, vx_recv.at[t, peer])

    source = q == r
    aside = jnp.logical_not(source)

    def seats(at):
        return pl.ds(pl.multiple_of(at * cols_tile, cols_tile), cols_tile)

    def vs_out(t, k):
        return remote(
            vt.at[t], vr.at[t, seats(j)], vs_send.at[t, k], vs_recv.at[t, j],
            r, q * ratio + (j + k) % ratio,
        )

    def vs_in(t, k):
        at = (j + k) % ratio
        spot = vr.at[t, seats(at)]
        return pltpu.make_async_copy(spot, spot, vs_recv.at[t, at])

    def vs_keep(t):
        return pltpu.make_async_copy(vt.at[t], vr.at[t, seats(j)], vl_sem.at[t])

    def v_each(t, act):
        for i in range(1, links):
            if t == 0:
                act(v_out(t, i))
            else:
                @pl.when((q + i) % links != r)
                def _():
                    act(v_out(t, i))
        if t == 0:
            for k in range(1, ratio):
                act(v_side(t, 0, k))
        else:
            @pl.when(aside)
            def _():
                for k in range(1, ratio):
                    act(v_side(t, 0, k))

    def v_direct(t):
        for i in range(1, links):
            v_in(t, ((q + i) % links) * ratio + j).wait()
            for k in range(1, ratio):
                v_side(t, i, k).start()
        for i in range(links):
            for k in range(1, ratio):
                v_in(t, ((q + i) % links) * ratio + (j + k) % ratio).wait()

    closed, gathered = set(), set()

    def v_gather(t):
        if t == 0:
            v_direct(t)
            return

        gathered.add(t)

        @pl.when(aside)
        def _():
            v_direct(t)

        @pl.when(source)
        def _():
            if t not in closed:
                vt_arrive(t)
            vs_keep(t).start()
            for k in range(1, ratio):
                vs_out(t, k).start()
            for k in range(1, ratio):
                vs_in(t, k).wait()
            vs_keep(t).wait()

    def vt_spread(t):
        @pl.when(stays)
        def _():
            vt_in(t).wait()

        @pl.when(jnp.logical_not(stays))
        def _():
            vt_move(t).wait()

        for i in range(1, nrow):
            vt_out(t, i).start()

    def vt_arrive(t):
        for i in range(1, nrow):
            vt_got(t, (r + i) % nrow).wait()

    def vt_close(t):
        if t in gathered:
            @pl.when(aside)
            def _():
                vt_arrive(t)
        else:
            vt_arrive(t)
            closed.add(t)
        vtt[t] = vt[t].astype(jnp.float32).T.astype(jnp.bfloat16)

    def rs_out(t, i):
        peer = (r + i) % nrow
        return remote(
            sent.at[t, peer], got.at[t, r], rs_send.at[t, i], rs_recv.at[t, r], peer, c
        )

    def rs_in(t, peer):
        return pltpu.make_async_copy(sent.at[t, peer], got.at[t, peer], rs_recv.at[t, peer])

    def wc_out(t, i):
        spot = wcc.at[t, r]
        return remote(spot, spot, wc_send.at[t, i], wc_recv.at[t, r], (r + i) % nrow, c)

    def wc_in(t, peer):
        spot = wcc.at[t, peer]
        return pltpu.make_async_copy(spot, spot, wc_recv.at[t, peer])

    def wr_out(t, i):
        return remote(
            wcc.at[t, r], wrc.at[t, j, r], wr_send.at[t, i], wr_recv.at[t, r],
            q, ((q + i) % links) * ratio + j,
        )

    def wr_in(t, peer):
        spot = wrc.at[t, j, peer]
        return pltpu.make_async_copy(spot, spot, wr_recv.at[t, peer])

    def wr_keep(t):
        return pltpu.make_async_copy(wcc.at[t], wrc.at[t, j], local_sem.at[t])

    def wx_out(t, k):
        spot = wrc.at[t, j]
        return remote(
            spot, spot, wx_send.at[t, k], wx_recv.at[t, j], r, q * ratio + (j + k) % ratio
        )

    def wx_in(t, k):
        at = (j + k) % ratio
        spot = wrc.at[t, at]
        return pltpu.make_async_copy(spot, spot, wx_recv.at[t, at])

    def partial(t):
        v_gather(t)
        part[t] = dot(vr[t], ab[0], TN) + dot(vr[t], ab[1], TN)
        for i in range(1, nrow):
            peer = (r + i) % nrow
            encode(sent.at[t, peer], part[t, strips(peer)])
            rs_out(t, i).start()

    def collect(t):
        total = part[t, strips(r)]
        for i in range(1, nrow):
            peer = (r + i) % nrow
            rs_in(t, peer).wait()
            total = total + decode(got.at[t, peer], strip)
        total = total * scaling
        encode(wcc.at[t, r], total)
        own[t, 0], own[t, 1] = halves(total)

    def spread(t):
        for i in range(1, nrow):
            wc_out(t, i).start()
        for i in range(1, links):
            wr_out(t, i).start()

    def relay(t):
        for i in range(1, nrow):
            wc_in(t, (r + i) % nrow).wait()

        @pl.when(source)
        def _():
            wr_keep(t).start()
            wr_keep(t).wait()

        @pl.when(jnp.logical_not(source))
        def _():
            for i in range(nrow):
                wr_in(t, (r + i) % nrow).wait()

        for k in range(1, ratio):
            wx_out(t, k).start()

    def open_cols(t):
        for k in range(nrow):
            at = pl.ds(k * strip, strip)
            wct[t, 0, at], wct[t, 1, at] = halves(decode(wcc.at[t, k], strip))

    def open_rows(t):
        for k in range(1, ratio):
            wx_in(t, k).wait()
        for s in range(ratio):
            x = jnp.concatenate([decode(wrc.at[t, s, k], strip) for k in range(nrow)], axis=0)
            at = pl.ds(s * cols_tile, cols_tile)
            wr[t, 0, at], wr[t, 1, at] = halves(x.T)

    def ga_out(k, s):
        to = (j + s) % ratio
        return remote(
            gp.at[k, :, thins(to)], ga.at[k, j], ga_send.at[k, s], ga_recv.at[k, j],
            r, q * ratio + to,
        )

    def ga_in(k, s):
        at = (j + s) % ratio
        return pltpu.make_async_copy(ga.at[k, at], ga.at[k, at], ga_recv.at[k, at])

    def gb_out(k, s):
        far = 2**s
        to = q + far - 2 * far * ((q // far) % 2)
        return remote(
            gs.at[k, s], gc.at[k, s], gb_send.at[k, s], gb_recv.at[k, s], r, to * ratio + j
        )

    def gb_in(k, s):
        return pltpu.make_async_copy(gc.at[k, s], gc.at[k, s], gb_recv.at[k, s])

    def gd_out(k, i):
        spot = gq.at[k, j, r]
        return remote(spot, spot, gd_send.at[k, i], gd_recv.at[k, r], (r + i) % nrow, c)

    def gd_in(k, i):
        at = (r + i) % nrow
        spot = gq.at[k, j, at]
        return pltpu.make_async_copy(spot, spot, gd_recv.at[k, at])

    def ge_out(k, s):
        spot = gq.at[k, j]
        return remote(
            spot, spot, ge_send.at[k, s], ge_recv.at[k, j], r, q * ratio + (j + s) % ratio
        )

    def ge_in(k, s):
        at = (j + s) % ratio
        spot = gq.at[k, at]
        return pltpu.make_async_copy(spot, spot, ge_recv.at[k, at])

    def gram_a(k):
        for m, (u, t) in enumerate(chosen):
            gp[k, m] = dot4(own.at[u], vt[t], NN) if k else dot(vtt[u, strips(r)], vt[t], NN)
        for s in range(1, ratio):
            ga_out(k, s).start()

    def gram_b(k):
        for s in range(1, ratio):
            ga_in(k, s).wait()
        totals = []
        for m in range(pairs):
            total = gp[k, m, thins(j)]
            for s in range(1, ratio):
                total = total + ga[k, (j + s) % ratio, m]
            gt[k, m] = total
            totals.append(total)
        encode_all(gs.at[k, 0], totals)
        gb_out(k, 0).start()

    def gram_add(k, s):
        gb_in(k, s).wait()
        totals = []
        for m in range(pairs):
            total = gt[k, m] + decode(gc.at[k, s], thin, m * thin)
            gt[k, m] = total
            totals.append(total)
        return totals

    def gram_c(k):
        for s in range(1, steps):
            encode_all(gs.at[k, s], gram_add(k, s - 1))
            gb_out(k, s).start()

    def gram_d(k):
        encode_all(gq.at[k, j, r], gram_add(k, steps - 1))
        for i in range(1, nrow):
            gd_out(k, i).start()

    def gram_e(k):
        for i in range(1, nrow):
            gd_in(k, i).wait()
        for s in range(1, ratio):
            ge_out(k, s).start()

    def gram_f(k):
        for s in range(1, ratio):
            ge_in(k, s).wait()
        for m in range(pairs):
            for i in range(nrow):
                for s in range(ratio):
                    at = pl.ds(i * strip + s * thin, thin)
                    gram[k, m, at] = decode(gq.at[k, s, i], thin, m * thin)

    def keep(k, m, x):
        fact[k, m, 0], fact[k, m, 1] = halves(x)

    def kept(k, m):
        return fact[k, m, 0], fact[k, m, 1]

    def make_c():
        keep(0, 0, -fix * gram[0, 0])
        keep(0, 2, -fix * gram[0, 2])
        keep(0, 1, dot2(kept(0, 0), kept(0, 2), NN) - fix * gram[0, 1])

    def make_d():
        keep(1, 0, -fix * gram[1, 0])
        keep(1, 1, dot2(kept(1, 0), kept(0, 2), NN) - fix * gram[1, 1])
        last = (
            gram[1, 2]
            + dot2(kept(0, 0), halves(gram[1, 1]), TN)
            + dot2(kept(1, 0), halves(gram[0, 1]), TN)
        )
        keep(1, 2, -fix * last)

    def both(x):
        return x[0], x[1]

    def full(x):
        return x[0].astype(jnp.float32) + x[1].astype(jnp.float32)

    def make_z():
        zt[0, 0], zt[0, 1] = halves(
            vtt[0].astype(jnp.float32)
            + dot4(kept(0, 0), vtt[1], NN) + dot4(kept(0, 1), vtt[2], NN)
        )
        zt[1, 0], zt[1, 1] = halves(vtt[1].astype(jnp.float32) + dot4(kept(0, 2), vtt[2], NN))

    def minus(terms):
        out_ref[...] = out_ref[...] - half * terms


    vt_start(1)
    vt_start(2)
    a_in.wait()
    ab[0], ab[1] = halves(a_ref[...])
    out_ref[...] = a_ref[...]
    v_each(1, start)
    vt_start(0)
    vt_spread(1)
    v_each(0, start)
    vt_spread(2)
    vt_spread(0)
    partial(1)
    v_each(2, start)
    partial(0)
    vt_close(2)
    vt_close(1)
    vt_close(0)
    gram_a(0)
    collect(1)
    spread(1)
    gram_b(0)
    collect(0)
    spread(0)
    gram_c(0)
    gram_a(1)
    gram_b(1)
    partial(2)
    gram_d(0)
    relay(0)
    relay(1)
    gram_c(1)
    collect(2)
    open_rows(0)
    spread(2)
    gram_d(1)
    open_rows(1)
    gram_e(0)
    gram_f(0)
    make_c()
    open_cols(1)
    make_z()
    relay(2)
    open_cols(0)
    minus(dot2(both(wr.at[0]), both(zt.at[0]), NN))
    open_rows(2)
    open_cols(2)
    gram_e(1)
    minus(dot2(both(wr.at[1]), both(zt.at[1]), NN))
    part[1] = full(wct.at[1]) + dot2(kept(0, 0), both(wct.at[0]), TN)
    part[2] = (
        full(wct.at[2]) + dot2(kept(0, 1), both(wct.at[0]), TN)
        + dot2(kept(0, 2), both(wct.at[1]), TN)
    )
    gram_f(1)
    make_d()
    zero = full(wct.at[0]) + dot4(kept(1, 0), vtt[1], NN) + dot4(kept(1, 1), vtt[2], NN)
    minus(dot3(vr[0], halves(zero), NN))
    one = part[1] + dot4(kept(1, 0), vtt[0], TN) + dot4(kept(1, 2), vtt[2], NN)
    minus(dot3(vr[1], halves(one), NN))
    two = part[2] + dot4(kept(1, 1), vtt[0], TN) + dot4(kept(1, 2), vtt[1], TN)
    minus(dot3(vr[2], halves(two), NN))
    minus(dot4(both(wr.at[2]), vtt[2], NN))
    mine = rows(c)
    for t in range(ticks):
        total = wr[t, 0, mine].astype(jnp.float32) + wr[t, 1, mine].astype(jnp.float32)
        for m, (u, later) in enumerate(chosen):
            if later == t:
                total = total + dot2((wr[u, 0, mine], wr[u, 1, mine]), kept(0, m), NN)
                total = total + dot3(vr[u, mine], kept(1, m), NN)
        w_ref[t] = total

    for t in range(ticks):
        v_each(t, wait_send)
        for i in range(1, links):
            wr_out(t, i).wait_send()
        for k in range(1, ratio):
            if t == 0:
                for i in range(1, links):
                    v_side(t, i, k).wait_send()
            else:
                @pl.when(aside)
                def _():
                    for i in range(1, links):
                        v_side(t, i, k).wait_send()

                @pl.when(source)
                def _():
                    vs_out(t, k).wait_send()
            wx_out(t, k).wait_send()
        for i in range(1, nrow):
            vt_out(t, i).wait_send()
            rs_out(t, i).wait_send()
            wc_out(t, i).wait_send()

    for k in range(2):
        for s in range(1, ratio):
            ga_out(k, s).wait_send()
            ge_out(k, s).wait_send()
        for s in range(steps):
            gb_out(k, s).wait_send()
        for i in range(1, nrow):
            gd_out(k, i).wait_send()


def on_device(trailing, v_panels):
    nrow = lax.axis_size("row")
    ncol = lax.axis_size("col")
    rows_tile, cols_tile = trailing.shape
    ticks, piece, depth = v_panels.shape
    ratio = rows_tile // cols_tile
    links = ncol // ratio
    scaling = 1.0 / math.sqrt(rows_tile * nrow)
    pairs = ticks * (ticks - 1) // 2
    strip = depth // nrow
    thin = strip // ratio
    steps = links.bit_length() - 1
    dma = pltpu.SemaphoreType.DMA
    vmem = pl.BlockSpec(memory_space=pltpu.VMEM)
    f32, bf16 = jnp.float32, jnp.bfloat16
    return pl.pallas_call(
        functools.partial(kernel, nrow, ncol, ratio, scaling),
        out_shape=(
            jax.ShapeDtypeStruct(trailing.shape, f32),
            jax.ShapeDtypeStruct(v_panels.shape, f32),
        ),
        in_specs=[pl.BlockSpec(memory_space=pltpu.MemorySpace.HBM)] * 2,
        out_specs=(vmem, vmem),
        scratch_shapes=[
            pltpu.VMEM((rows_tile, cols_tile), f32),
            pltpu.VMEM((2, rows_tile, cols_tile), bf16),
            pltpu.VMEM((ticks, piece, depth), bf16),
            pltpu.VMEM((ticks, rows_tile, depth), bf16),
            pltpu.VMEM((ticks, cols_tile, depth), bf16),
            pltpu.VMEM((ticks, depth, cols_tile), bf16),
            pltpu.VMEM((ticks, depth, cols_tile), f32),
            pltpu.VMEM((ticks, nrow, strip + TILE, cols_tile), bf16),
            pltpu.VMEM((ticks, nrow, strip + TILE, cols_tile), bf16),
            pltpu.VMEM((ticks, 2, strip, cols_tile), bf16),
            pltpu.VMEM((ticks, nrow, strip + TILE, cols_tile), bf16),
            pltpu.VMEM((ticks, ratio, nrow, strip + TILE, cols_tile), bf16),
            pltpu.VMEM((ticks, 2, depth, cols_tile), bf16),
            pltpu.VMEM((ticks, 2, rows_tile, depth), bf16),
            pltpu.VMEM((ticks - 1, 2, depth, cols_tile), bf16),
            pltpu.VMEM((2, pairs, strip, depth), f32),
            pltpu.VMEM((2, pairs, thin, depth), f32),
            pltpu.VMEM((2, ratio, pairs, thin, depth), f32),
            pltpu.VMEM((2, steps, pairs * thin + TILE, depth), bf16),
            pltpu.VMEM((2, steps, pairs * thin + TILE, depth), bf16),
            pltpu.VMEM((2, ratio, nrow, pairs * thin + TILE, depth), bf16),
            pltpu.VMEM((2, pairs, depth, depth), f32),
            pltpu.VMEM((2, pairs, 2, depth, depth), bf16),
            dma((ticks, links)),
            dma((ticks, ncol)),
            dma((ticks,)),
            dma((ticks,)),
            dma((ticks, links, ratio)),
            dma((ticks, nrow)),
            dma((ticks, nrow)),
            dma((ticks, ratio)),
            dma((ticks, ratio)),
            dma((ticks,)),
            dma((ticks, nrow)),
            dma((ticks, nrow)),
            dma((ticks, nrow)),
            dma((ticks, nrow)),
            dma((ticks, links)),
            dma((ticks, nrow)),
            dma((ticks, ratio)),
            dma((ticks, ratio)),
            dma((ticks,)),
            dma((3,)),
            dma((2, ratio)), dma((2, ratio)),
            dma((2, steps)), dma((2, steps)),
            dma((2, nrow)), dma((2, nrow)),
            dma((2, ratio)), dma((2, ratio)),
        ],
        compiler_params=pltpu.CompilerParams(
            collective_id=0, has_side_effects=True, vmem_limit_bytes=48 * 1024 * 1024
        ),
    )(trailing, v_panels)


def solution(mesh):
    in_specs = (P("row", "col"), P(None, ("row", "col"), None))
    out_specs = (P("row", "col"), P(None, ("row", "col"), None))
    return jax.shard_map(
        on_device, mesh=mesh, in_specs=in_specs, out_specs=out_specs, check_vma=False
    )
```

```python
import functools
import math

import jax
import jax.numpy as jnp
from jax import lax
from jax.experimental import pallas as pl
from jax.experimental.pallas import tpu as pltpu
from jax.sharding import PartitionSpec as P

MESH = pl.DeviceIdType.MESH
NT = (((1,), (1,)), ((), ()))
NN = (((1,), (0,)), ((), ()))
TN = (((0,), (0,)), ((), ()))
SPAN = 124.0
TINY = 1e-30
TILE = 8
DIRECT = ()


def dot(a, b, dims):
    return lax.dot_general(a, b, dims, preferred_element_type=jnp.float32)


def halves(x):
    high = x.astype(jnp.bfloat16)
    return high, (x - high.astype(jnp.float32)).astype(jnp.bfloat16)


def dot2(a, b, dims):
    return dot(a[0], b[0], dims) + (dot(a[0], b[1], dims) + dot(a[1], b[0], dims))


def dot3(a, b, dims):
    return dot(a, b[0], dims) + dot(a, b[1], dims)


def dot4(a, b, dims):
    return dot(a[0], b, dims) + dot(a[1], b, dims)


def fold(x):
    width = x.shape[1] // 2
    return x[:, :width] + x[:, width:]


def wide(pair):
    return jnp.concatenate(pair, axis=1)


def encode(ref, x):
    rows = x.shape[0]
    peak = jnp.maximum(jnp.max(jnp.abs(x), axis=0, keepdims=True), TINY).astype(jnp.bfloat16)
    ref[pl.ds(0, rows)] = jnp.exp2(x * (SPAN / peak.astype(jnp.float32))).astype(jnp.bfloat16)
    ref[pl.ds(ref.shape[0] - TILE, TILE)] = jnp.broadcast_to(peak, (TILE, x.shape[1]))


def encode_all(ref, parts):
    rows = parts[0].shape[0]
    peak = jnp.max(jnp.abs(parts[0]), axis=0, keepdims=True)
    for x in parts[1:]:
        peak = jnp.maximum(peak, jnp.max(jnp.abs(x), axis=0, keepdims=True))
    peak = jnp.maximum(peak, TINY).astype(jnp.bfloat16)
    scale = SPAN / peak.astype(jnp.float32)
    for i, x in enumerate(parts):
        ref[pl.ds(i * rows, rows)] = jnp.exp2(x * scale).astype(jnp.bfloat16)
    ref[pl.ds(ref.shape[0] - TILE, TILE)] = jnp.broadcast_to(peak, (TILE, peak.shape[1]))


def decode(ref, rows, at=0):
    peak = ref[pl.ds(ref.shape[0] - TILE, TILE)].astype(jnp.float32)[:1]
    return jnp.log2(ref[pl.ds(at, rows)].astype(jnp.float32)) * (peak * (1.0 / SPAN))


def kernel(
    nrow, ncol, ratio, scaling,
    a_hbm, v_ref, out_ref, w_ref,
    a_ref, ab, vo, vr, vt, vtt, part, sent, got, own, wcc, wrc, wct, wr, zt, gp, gt, ga, gs, gc, gq, gram, fact,
    v_send, v_recv, vt_send, vt_recv, vx_send, vo_send, vx_recv, vs_send, vs_recv, vl_sem,
    rs_send, rs_recv, wc_send, wc_recv, wr_send, wr_recv, wx_send, wx_recv, local_sem, in_sem,
    ga_send, ga_recv, gb_send, gb_recv, gd_send, gd_recv, ge_send, ge_recv,
):
    ticks, piece, depth = v_ref.shape
    rows_tile, cols_tile = a_hbm.shape
    links = ncol // ratio
    chosen = [(u, t) for t in range(ticks) for u in range(t)]
    pairs = len(chosen)
    r = lax.axis_index("row")
    c = lax.axis_index("col")
    q = c // ratio
    j = c % ratio
    half = 0.5 * scaling
    fix = scaling * half
    strip = depth // nrow
    thin = strip // ratio
    steps = gs.shape[1]

    def rows(at):
        return pl.ds(pl.multiple_of(at * piece, piece), piece)

    def strips(at):
        return pl.ds(pl.multiple_of(at * strip, strip), strip)

    def thins(at):
        return pl.ds(pl.multiple_of(at * thin, thin), thin)

    def remote(src, dst, send, recv, row, col):
        return pltpu.make_async_remote_copy(
            src_ref=src, dst_ref=dst, send_sem=send, recv_sem=recv,
            device_id=(row, col), device_id_type=MESH,
        )

    from_row, from_col = c // ratio, j * nrow + r
    to_row, to_col = c % nrow, r * ratio + c // nrow
    stays = jnp.logical_and(to_row == r, to_col == c)

    a_in = pltpu.make_async_copy(a_hbm, a_ref, in_sem.at[0])
    v_own = pltpu.make_async_copy(v_ref, vr.at[:, rows(c)], in_sem.at[1])
    v_src = pltpu.make_async_copy(v_ref, vo, in_sem.at[2])
    v_src.start()
    v_own.start()
    a_in.start()
    barrier = pltpu.get_barrier_semaphore()

    def greet(row, col):
        pl.semaphore_signal(barrier, inc=1, device_id=(row, col), device_id_type=MESH)

    for i in range(1, nrow):
        greet((r + i) % nrow, c)
    for k in range(1, ratio):
        greet(r, q * ratio + (j + k) % ratio)
    for i in range(1, links):
        greet(r, ((q + i) % links) * ratio + j)

    @pl.when(jnp.logical_not(stays))
    def _():
        greet(from_row, from_col)
        greet(to_row, to_col)

    v_src.wait()
    v_own.wait()
    pl.semaphore_wait(barrier, nrow + ratio + links - 3 + jnp.where(stays, 0, 2))

    def start(copy):
        copy.start()

    def wait_send(copy):
        copy.wait_send()

    def v_out(t, i):
        return remote(
            vo.at[t], vr.at[t, rows(c)], v_send.at[t, i], v_recv.at[t, c],
            r, ((q + i) % links) * ratio + j,
        )

    def v_side(t, i, k):
        at = ((q + i) % links) * ratio + j
        spot = vr.at[t, rows(at)]
        return remote(
            spot if i else vo.at[t], spot, vx_send.at[t, i, k - 1], v_recv.at[t, at],
            r, q * ratio + (j + k) % ratio,
        )

    def v_in(t, col):
        spot = vr.at[t, rows(col)]
        return pltpu.make_async_copy(spot, spot, v_recv.at[t, col])

    def vt_move(t):
        return remote(
            vo.at[t], vt.at[t, rows(to_row)], vt_send.at[t], vt_recv.at[t], to_row, to_col
        )

    def vt_in(t):
        return pltpu.make_async_copy(vo.at[t], vt.at[t, rows(r)], vt_recv.at[t])

    def vt_start(t):
        @pl.when(stays)
        def _():
            vt_in(t).start()

        @pl.when(jnp.logical_not(stays))
        def _():
            vt_move(t).start()

    def vt_out(t, i):
        peer = (r + i) % nrow
        spot = vt.at[t, rows(r)]
        return remote(spot, spot, vo_send.at[t, i], vx_recv.at[t, r], peer, c)

    def vt_got(t, peer):
        spot = vt.at[t, rows(peer)]
        return pltpu.make_async_copy(spot, spot, vx_recv.at[t, peer])

    source = q == r
    aside = jnp.logical_not(source)

    def seats(at):
        return pl.ds(pl.multiple_of(at * cols_tile, cols_tile), cols_tile)

    def vs_out(t, k):
        return remote(
            vt.at[t], vr.at[t, seats(j)], vs_send.at[t, k], vs_recv.at[t, j],
            r, q * ratio + (j + k) % ratio,
        )

    def vs_in(t, k):
        at = (j + k) % ratio
        spot = vr.at[t, seats(at)]
        return pltpu.make_async_copy(spot, spot, vs_recv.at[t, at])

    def vs_keep(t):
        return pltpu.make_async_copy(vt.at[t], vr.at[t, seats(j)], vl_sem.at[t])

    def v_each(t, act):
        for i in range(1, links):
            if t in DIRECT:
                act(v_out(t, i))
            else:
                @pl.when((q + i) % links != r)
                def _():
                    act(v_out(t, i))
        if t in DIRECT:
            for k in range(1, ratio):
                act(v_side(t, 0, k))
        else:
            @pl.when(aside)
            def _():
                for k in range(1, ratio):
                    act(v_side(t, 0, k))

    def v_direct(t):
        for i in range(1, links):
            v_in(t, ((q + i) % links) * ratio + j).wait()
            for k in range(1, ratio):
                v_side(t, i, k).start()
        for i in range(links):
            for k in range(1, ratio):
                v_in(t, ((q + i) % links) * ratio + (j + k) % ratio).wait()

    closed, gathered = set(), set()

    def v_gather(t):
        if t in DIRECT:
            v_direct(t)
            return

        gathered.add(t)

        @pl.when(aside)
        def _():
            v_direct(t)

        @pl.when(source)
        def _():
            if t not in closed:
                vt_arrive(t)
            vs_keep(t).start()
            for k in range(1, ratio):
                vs_out(t, k).start()
            for k in range(1, ratio):
                vs_in(t, k).wait()
            vs_keep(t).wait()

    def vt_spread(t):
        @pl.when(stays)
        def _():
            vt_in(t).wait()

        @pl.when(jnp.logical_not(stays))
        def _():
            vt_move(t).wait()

        for i in range(1, nrow):
            vt_out(t, i).start()

    def vt_arrive(t):
        for i in range(1, nrow):
            vt_got(t, (r + i) % nrow).wait()

    def vt_close(t):
        if t in gathered:
            @pl.when(aside)
            def _():
                vt_arrive(t)
        else:
            vt_arrive(t)
            closed.add(t)
        vtt[t] = vt[t].astype(jnp.float32).T.astype(jnp.bfloat16)

    def rs_out(t, i):
        peer = (r + i) % nrow
        return remote(
            sent.at[t, peer], got.at[t, r], rs_send.at[t, i], rs_recv.at[t, r], peer, c
        )

    def rs_in(t, peer):
        return pltpu.make_async_copy(sent.at[t, peer], got.at[t, peer], rs_recv.at[t, peer])

    def wc_out(t, i):
        spot = wcc.at[t, r]
        return remote(spot, spot, wc_send.at[t, i], wc_recv.at[t, r], (r + i) % nrow, c)

    def wc_in(t, peer):
        spot = wcc.at[t, peer]
        return pltpu.make_async_copy(spot, spot, wc_recv.at[t, peer])

    def wr_out(t, i):
        return remote(
            wcc.at[t, r], wrc.at[t, j, r], wr_send.at[t, i], wr_recv.at[t, r],
            q, ((q + i) % links) * ratio + j,
        )

    def wr_in(t, peer):
        spot = wrc.at[t, j, peer]
        return pltpu.make_async_copy(spot, spot, wr_recv.at[t, peer])

    def wr_keep(t):
        return pltpu.make_async_copy(wcc.at[t], wrc.at[t, j], local_sem.at[t])

    def wx_out(t, k):
        spot = wrc.at[t, j]
        return remote(
            spot, spot, wx_send.at[t, k], wx_recv.at[t, j], r, q * ratio + (j + k) % ratio
        )

    def wx_in(t, k):
        at = (j + k) % ratio
        spot = wrc.at[t, at]
        return pltpu.make_async_copy(spot, spot, wx_recv.at[t, at])

    def partial(t):
        v_gather(t)
        part[t] = fold(dot(vr[t], ab[...], TN))
        for i in range(1, nrow):
            peer = (r + i) % nrow
            encode(sent.at[t, peer], part[t, strips(peer)])
            rs_out(t, i).start()

    def collect(t):
        total = part[t, strips(r)]
        for i in range(1, nrow):
            peer = (r + i) % nrow
            rs_in(t, peer).wait()
            total = total + decode(got.at[t, peer], strip)
        total = total * scaling
        encode(wcc.at[t, r], total)
        own[t, 0], own[t, 1] = halves(total)

    def spread(t):
        for i in range(1, nrow):
            wc_out(t, i).start()
        for i in range(1, links):
            wr_out(t, i).start()

    def relay(t):
        for i in range(1, nrow):
            wc_in(t, (r + i) % nrow).wait()

        @pl.when(source)
        def _():
            wr_keep(t).start()
            wr_keep(t).wait()

        @pl.when(jnp.logical_not(source))
        def _():
            for i in range(nrow):
                wr_in(t, (r + i) % nrow).wait()

        for k in range(1, ratio):
            wx_out(t, k).start()

    def open_cols(t):
        for k in range(nrow):
            at = pl.ds(k * strip, strip)
            wct[t, 0, at], wct[t, 1, at] = halves(decode(wcc.at[t, k], strip))

    def open_rows(t):
        for k in range(1, ratio):
            wx_in(t, k).wait()
        for s in range(ratio):
            x = jnp.concatenate([decode(wrc.at[t, s, k], strip) for k in range(nrow)], axis=0)
            at = pl.ds(s * cols_tile, cols_tile)
            wr[t, 0, at], wr[t, 1, at] = halves(x.T)

    def ga_out(k, s):
        to = (j + s) % ratio
        return remote(
            gp.at[k, :, thins(to)], ga.at[k, j], ga_send.at[k, s], ga_recv.at[k, j],
            r, q * ratio + to,
        )

    def ga_in(k, s):
        at = (j + s) % ratio
        return pltpu.make_async_copy(ga.at[k, at], ga.at[k, at], ga_recv.at[k, at])

    def gb_out(k, s):
        far = 2**s
        to = q + far - 2 * far * ((q // far) % 2)
        return remote(
            gs.at[k, s], gc.at[k, s], gb_send.at[k, s], gb_recv.at[k, s], r, to * ratio + j
        )

    def gb_in(k, s):
        return pltpu.make_async_copy(gc.at[k, s], gc.at[k, s], gb_recv.at[k, s])

    def gd_out(k, i):
        spot = gq.at[k, j, r]
        return remote(spot, spot, gd_send.at[k, i], gd_recv.at[k, r], (r + i) % nrow, c)

    def gd_in(k, i):
        at = (r + i) % nrow
        spot = gq.at[k, j, at]
        return pltpu.make_async_copy(spot, spot, gd_recv.at[k, at])

    def ge_out(k, s):
        spot = gq.at[k, j]
        return remote(
            spot, spot, ge_send.at[k, s], ge_recv.at[k, j], r, q * ratio + (j + s) % ratio
        )

    def ge_in(k, s):
        at = (j + s) % ratio
        spot = gq.at[k, at]
        return pltpu.make_async_copy(spot, spot, ge_recv.at[k, at])

    def gram_a(k):
        for m, (u, t) in enumerate(chosen):
            gp[k, m] = dot4(own.at[u], vt[t], NN) if k else dot(vtt[u, strips(r)], vt[t], NN)
        for s in range(1, ratio):
            ga_out(k, s).start()

    def gram_b(k):
        for s in range(1, ratio):
            ga_in(k, s).wait()
        totals = []
        for m in range(pairs):
            total = gp[k, m, thins(j)]
            for s in range(1, ratio):
                total = total + ga[k, (j + s) % ratio, m]
            gt[k, m] = total
            totals.append(total)
        encode_all(gs.at[k, 0], totals)
        gb_out(k, 0).start()

    def gram_add(k, s):
        gb_in(k, s).wait()
        totals = []
        for m in range(pairs):
            total = gt[k, m] + decode(gc.at[k, s], thin, m * thin)
            gt[k, m] = total
            totals.append(total)
        return totals

    def gram_c(k):
        for s in range(1, steps):
            encode_all(gs.at[k, s], gram_add(k, s - 1))
            gb_out(k, s).start()

    def gram_d(k):
        encode_all(gq.at[k, j, r], gram_add(k, steps - 1))
        for i in range(1, nrow):
            gd_out(k, i).start()

    def gram_e(k):
        for i in range(1, nrow):
            gd_in(k, i).wait()
        for s in range(1, ratio):
            ge_out(k, s).start()

    def gram_f(k):
        for s in range(1, ratio):
            ge_in(k, s).wait()
        for m in range(pairs):
            for i in range(nrow):
                for s in range(ratio):
                    at = pl.ds(i * strip + s * thin, thin)
                    gram[k, m, at] = decode(gq.at[k, s, i], thin, m * thin)

    def times(k, m, x):
        y = dot(fact[k, m].reshape(2 * depth, depth), x, NN)
        return y[:depth] + y[depth:]

    def keep(k, m, x):
        fact[k, m, 0], fact[k, m, 1] = halves(x)

    def kept(k, m):
        return fact[k, m, 0], fact[k, m, 1]

    def make_c():
        keep(0, 0, -fix * gram[0, 0])
        keep(0, 2, -fix * gram[0, 2])
        keep(0, 1, dot2(kept(0, 0), kept(0, 2), NN) - fix * gram[0, 1])

    def make_d():
        keep(1, 0, -fix * gram[1, 0])
        keep(1, 1, dot2(kept(1, 0), kept(0, 2), NN) - fix * gram[1, 1])
        last = (
            gram[1, 2]
            + dot2(kept(0, 0), halves(gram[1, 1]), TN)
            + dot2(kept(1, 0), halves(gram[0, 1]), TN)
        )
        keep(1, 2, -fix * last)

    def both(x):
        return x[0], x[1]

    def full(x):
        return x[0].astype(jnp.float32) + x[1].astype(jnp.float32)

    def make_z():
        zt[0, 0], zt[0, 1] = halves(
            vtt[0].astype(jnp.float32)
            + times(0, 0, vtt[1]) + times(0, 1, vtt[2])
        )
        zt[1, 0], zt[1, 1] = halves(vtt[1].astype(jnp.float32) + times(0, 2, vtt[2]))

    def minus(terms):
        out_ref[...] = out_ref[...] - half * terms


    vt_start(1)
    vt_start(2)
    a_in.wait()
    ab[...] = wide(halves(a_ref[...]))
    out_ref[...] = a_ref[...]
    vt_start(0)
    v_each(1, start)
    v_each(2, start)
    vt_spread(1)
    vt_spread(2)
    vt_spread(0)
    v_each(0, start)
    partial(1)
    vt_close(1)
    partial(2)
    partial(0)
    vt_close(0)
    vt_close(2)
    gram_a(0)
    gram_b(0)
    collect(1)
    spread(1)
    collect(0)
    gram_a(1)
    gram_c(0)
    gram_b(1)
    collect(2)
    spread(0)
    gram_c(1)
    relay(1)
    gram_d(0)
    open_rows(1)
    spread(2)
    relay(0)
    gram_d(1)
    gram_e(0)
    gram_f(0)
    make_c()
    open_rows(0)
    make_z()
    relay(2)
    open_cols(1)
    open_cols(2)
    open_cols(0)
    minus(fold(dot(wr[1, 0], wide(both(zt.at[1])), NN)) + dot(wr[1, 1], zt[1, 0], NN))
    part[1] = full(wct.at[1]) + dot2(kept(0, 0), both(wct.at[0]), TN)
    part[2] = (
        full(wct.at[2]) + dot2(kept(0, 1), both(wct.at[0]), TN)
        + dot2(kept(0, 2), both(wct.at[1]), TN)
    )
    gram_e(1)
    open_rows(2)
    minus(fold(dot(wr[0, 0], wide(both(zt.at[0])), NN)) + dot(wr[0, 1], zt[0, 0], NN))
    gram_f(1)
    make_d()
    zero = full(wct.at[0]) + times(1, 0, vtt[1]) + times(1, 1, vtt[2])
    minus(fold(dot(vr[0], wide(halves(zero)), NN)))
    one = part[1] + dot4(kept(1, 0), vtt[0], TN) + times(1, 2, vtt[2])
    minus(fold(dot(vr[1], wide(halves(one)), NN)))
    two = part[2] + dot4(kept(1, 1), vtt[0], TN) + dot4(kept(1, 2), vtt[1], TN)
    minus(fold(dot(vr[2], wide(halves(two)), NN)))
    minus(dot4(both(wr.at[2]), vtt[2], NN))
    mine = rows(c)
    for t in range(ticks):
        total = wr[t, 0, mine].astype(jnp.float32) + wr[t, 1, mine].astype(jnp.float32)
        for m, (u, later) in enumerate(chosen):
            if later == t:
                total = total + dot2((wr[u, 0, mine], wr[u, 1, mine]), kept(0, m), NN)
                total = total + dot3(vr[u, mine], kept(1, m), NN)
        w_ref[t] = total

    for t in range(ticks):
        v_each(t, wait_send)
        for i in range(1, links):
            wr_out(t, i).wait_send()
        for k in range(1, ratio):
            if t in DIRECT:
                for i in range(1, links):
                    v_side(t, i, k).wait_send()
            else:
                @pl.when(aside)
                def _():
                    for i in range(1, links):
                        v_side(t, i, k).wait_send()

                @pl.when(source)
                def _():
                    vs_out(t, k).wait_send()
            wx_out(t, k).wait_send()
        for i in range(1, nrow):
            vt_out(t, i).wait_send()
            rs_out(t, i).wait_send()
            wc_out(t, i).wait_send()

    for k in range(2):
        for s in range(1, ratio):
            ga_out(k, s).wait_send()
            ge_out(k, s).wait_send()
        for s in range(steps):
            gb_out(k, s).wait_send()
        for i in range(1, nrow):
            gd_out(k, i).wait_send()


def on_device(trailing, v_panels):
    nrow = lax.axis_size("row")
    ncol = lax.axis_size("col")
    rows_tile, cols_tile = trailing.shape
    ticks, piece, depth = v_panels.shape
    ratio = rows_tile // cols_tile
    links = ncol // ratio
    scaling = 1.0 / math.sqrt(rows_tile * nrow)
    pairs = ticks * (ticks - 1) // 2
    strip = depth // nrow
    thin = strip // ratio
    steps = links.bit_length() - 1
    dma = pltpu.SemaphoreType.DMA
    vmem = pl.BlockSpec(memory_space=pltpu.VMEM)
    f32, bf16 = jnp.float32, jnp.bfloat16
    return pl.pallas_call(
        functools.partial(kernel, nrow, ncol, ratio, scaling),
        out_shape=(
            jax.ShapeDtypeStruct(trailing.shape, f32),
            jax.ShapeDtypeStruct(v_panels.shape, f32),
        ),
        in_specs=[pl.BlockSpec(memory_space=pltpu.MemorySpace.HBM)] * 2,
        out_specs=(vmem, vmem),
        scratch_shapes=[
            pltpu.VMEM((rows_tile, cols_tile), f32),
            pltpu.VMEM((rows_tile, 2 * cols_tile), bf16),
            pltpu.VMEM((ticks, piece, depth), bf16),
            pltpu.VMEM((ticks, rows_tile, depth), bf16),
            pltpu.VMEM((ticks, cols_tile, depth), bf16),
            pltpu.VMEM((ticks, depth, cols_tile), bf16),
            pltpu.VMEM((ticks, depth, cols_tile), f32),
            pltpu.VMEM((ticks, nrow, strip + TILE, cols_tile), bf16),
            pltpu.VMEM((ticks, nrow, strip + TILE, cols_tile), bf16),
            pltpu.VMEM((ticks, 2, strip, cols_tile), bf16),
            pltpu.VMEM((ticks, nrow, strip + TILE, cols_tile), bf16),
            pltpu.VMEM((ticks, ratio, nrow, strip + TILE, cols_tile), bf16),
            pltpu.VMEM((ticks, 2, depth, cols_tile), bf16),
            pltpu.VMEM((ticks, 2, rows_tile, depth), bf16),
            pltpu.VMEM((ticks - 1, 2, depth, cols_tile), bf16),
            pltpu.VMEM((2, pairs, strip, depth), f32),
            pltpu.VMEM((2, pairs, thin, depth), f32),
            pltpu.VMEM((2, ratio, pairs, thin, depth), f32),
            pltpu.VMEM((2, steps, pairs * thin + TILE, depth), bf16),
            pltpu.VMEM((2, steps, pairs * thin + TILE, depth), bf16),
            pltpu.VMEM((2, ratio, nrow, pairs * thin + TILE, depth), bf16),
            pltpu.VMEM((2, pairs, depth, depth), f32),
            pltpu.VMEM((2, pairs, 2, depth, depth), bf16),
            dma((ticks, links)),
            dma((ticks, ncol)),
            dma((ticks,)),
            dma((ticks,)),
            dma((ticks, links, ratio)),
            dma((ticks, nrow)),
            dma((ticks, nrow)),
            dma((ticks, ratio)),
            dma((ticks, ratio)),
            dma((ticks,)),
            dma((ticks, nrow)),
            dma((ticks, nrow)),
            dma((ticks, nrow)),
            dma((ticks, nrow)),
            dma((ticks, links)),
            dma((ticks, nrow)),
            dma((ticks, ratio)),
            dma((ticks, ratio)),
            dma((ticks,)),
            dma((3,)),
            dma((2, ratio)), dma((2, ratio)),
            dma((2, steps)), dma((2, steps)),
            dma((2, nrow)), dma((2, nrow)),
            dma((2, ratio)), dma((2, ratio)),
        ],
        compiler_params=pltpu.CompilerParams(
            collective_id=0, has_side_effects=True, vmem_limit_bytes=48 * 1024 * 1024
        ),
    )(trailing, v_panels)


def solution(mesh):
    in_specs = (P("row", "col"), P(None, ("row", "col"), None))
    out_specs = (P("row", "col"), P(None, ("row", "col"), None))
    return jax.shard_map(
        on_device, mesh=mesh, in_specs=in_specs, out_specs=out_specs, check_vma=False
    )
```

```python
import functools
import math

import jax
import jax.numpy as jnp
from jax import lax
from jax.experimental import pallas as pl
from jax.experimental.pallas import tpu as pltpu
from jax.sharding import PartitionSpec as P

MESH = pl.DeviceIdType.MESH
NT = (((1,), (1,)), ((), ()))
NN = (((1,), (0,)), ((), ()))
TN = (((0,), (0,)), ((), ()))
SPAN = 124.0
TINY = 1e-30
TILE = 8
DIRECT = ()


def dot(a, b, dims):
    return lax.dot_general(a, b, dims, preferred_element_type=jnp.float32)


def halves(x):
    high = x.astype(jnp.bfloat16)
    return high, (x - high.astype(jnp.float32)).astype(jnp.bfloat16)


def dot2(a, b, dims):
    return dot(a[0], b[0], dims) + (dot(a[0], b[1], dims) + dot(a[1], b[0], dims))


def dot3(a, b, dims):
    return dot(a, b[0], dims) + dot(a, b[1], dims)


def dot4(a, b, dims):
    return dot(a[0], b, dims) + dot(a[1], b, dims)


def fold(x):
    width = x.shape[1] // 2
    return x[:, :width] + x[:, width:]


def wide(pair):
    return jnp.concatenate(pair, axis=1)


def encode(ref, x):
    rows = x.shape[0]
    peak = jnp.maximum(jnp.max(jnp.abs(x), axis=0, keepdims=True), TINY).astype(jnp.bfloat16)
    ref[pl.ds(0, rows)] = jnp.exp2(x * (SPAN / peak.astype(jnp.float32))).astype(jnp.bfloat16)
    ref[pl.ds(ref.shape[0] - TILE, TILE)] = jnp.broadcast_to(peak, (TILE, x.shape[1]))


def encode_all(ref, parts):
    rows = parts[0].shape[0]
    peak = jnp.max(jnp.abs(parts[0]), axis=0, keepdims=True)
    for x in parts[1:]:
        peak = jnp.maximum(peak, jnp.max(jnp.abs(x), axis=0, keepdims=True))
    peak = jnp.maximum(peak, TINY).astype(jnp.bfloat16)
    scale = SPAN / peak.astype(jnp.float32)
    for i, x in enumerate(parts):
        ref[pl.ds(i * rows, rows)] = jnp.exp2(x * scale).astype(jnp.bfloat16)
    ref[pl.ds(ref.shape[0] - TILE, TILE)] = jnp.broadcast_to(peak, (TILE, peak.shape[1]))


def decode(ref, rows, at=0):
    peak = ref[pl.ds(ref.shape[0] - TILE, TILE)].astype(jnp.float32)[:1]
    return jnp.log2(ref[pl.ds(at, rows)].astype(jnp.float32)) * (peak * (1.0 / SPAN))


def kernel(
    nrow, ncol, ratio, scaling,
    a_hbm, v_ref, out_ref, w_ref,
    a_ref, ab, vo, vr, vt, vtt, part, sent, got, own, wcc, wrc, wct, wr, zt, gp, gt, ga, gs, gc, gq, gram, fact,
    v_send, v_recv, vt_send, vt_recv, vx_send, vo_send, vx_recv, vs_send, vs_recv, vl_sem,
    rs_send, rs_recv, wc_send, wc_recv, wr_send, wr_recv, wx_send, wx_recv, local_sem, in_sem,
    ga_send, ga_recv, gb_send, gb_recv, gd_send, gd_recv, ge_send, ge_recv,
):
    ticks, piece, depth = v_ref.shape
    rows_tile, cols_tile = a_hbm.shape
    links = ncol // ratio
    chosen = [(u, t) for t in range(ticks) for u in range(t)]
    pairs = len(chosen)
    r = lax.axis_index("row")
    c = lax.axis_index("col")
    q = c // ratio
    j = c % ratio
    half = 0.5 * scaling
    fix = scaling * half
    strip = depth // nrow
    thin = strip // ratio
    steps = gs.shape[1]

    def rows(at):
        return pl.ds(pl.multiple_of(at * piece, piece), piece)

    def strips(at):
        return pl.ds(pl.multiple_of(at * strip, strip), strip)

    def thins(at):
        return pl.ds(pl.multiple_of(at * thin, thin), thin)

    def remote(src, dst, send, recv, row, col):
        return pltpu.make_async_remote_copy(
            src_ref=src, dst_ref=dst, send_sem=send, recv_sem=recv,
            device_id=(row, col), device_id_type=MESH,
        )

    from_row, from_col = c // ratio, j * nrow + r
    to_row, to_col = c % nrow, r * ratio + c // nrow
    stays = jnp.logical_and(to_row == r, to_col == c)

    a_in = pltpu.make_async_copy(a_hbm, a_ref, in_sem.at[0])
    v_own = pltpu.make_async_copy(v_ref, vr.at[:, rows(c)], in_sem.at[1])
    v_src = pltpu.make_async_copy(v_ref, vo, in_sem.at[2])
    v_src.start()
    v_own.start()
    a_in.start()
    barrier = pltpu.get_barrier_semaphore()

    def greet(row, col):
        pl.semaphore_signal(barrier, inc=1, device_id=(row, col), device_id_type=MESH)

    for i in range(1, nrow):
        greet((r + i) % nrow, c)
    for k in range(1, ratio):
        greet(r, q * ratio + (j + k) % ratio)
    for i in range(1, links):
        greet(r, ((q + i) % links) * ratio + j)

    @pl.when(jnp.logical_not(stays))
    def _():
        greet(from_row, from_col)
        greet(to_row, to_col)

    v_src.wait()
    v_own.wait()
    pl.semaphore_wait(barrier, nrow + ratio + links - 3 + jnp.where(stays, 0, 2))

    def start(copy):
        copy.start()

    def wait_send(copy):
        copy.wait_send()

    def v_out(t, i):
        return remote(
            vo.at[t], vr.at[t, rows(c)], v_send.at[t, i], v_recv.at[t, c],
            r, ((q + i) % links) * ratio + j,
        )

    def v_side(t, i, k):
        at = ((q + i) % links) * ratio + j
        spot = vr.at[t, rows(at)]
        return remote(
            spot if i else vo.at[t], spot, vx_send.at[t, i, k - 1], v_recv.at[t, at],
            r, q * ratio + (j + k) % ratio,
        )

    def v_in(t, col):
        spot = vr.at[t, rows(col)]
        return pltpu.make_async_copy(spot, spot, v_recv.at[t, col])

    def vt_move(t):
        return remote(
            vo.at[t], vt.at[t, rows(to_row)], vt_send.at[t], vt_recv.at[t], to_row, to_col
        )

    def vt_in(t):
        return pltpu.make_async_copy(vo.at[t], vt.at[t, rows(r)], vt_recv.at[t])

    def vt_start(t):
        @pl.when(stays)
        def _():
            vt_in(t).start()

        @pl.when(jnp.logical_not(stays))
        def _():
            vt_move(t).start()

    def vt_out(t, i):
        peer = (r + i) % nrow
        spot = vt.at[t, rows(r)]
        return remote(spot, spot, vo_send.at[t, i], vx_recv.at[t, r], peer, c)

    def vt_got(t, peer):
        spot = vt.at[t, rows(peer)]
        return pltpu.make_async_copy(spot, spot, vx_recv.at[t, peer])

    source = q == r
    aside = jnp.logical_not(source)

    def seats(at):
        return pl.ds(pl.multiple_of(at * cols_tile, cols_tile), cols_tile)

    def vs_out(t, k):
        return remote(
            vt.at[t], vr.at[t, seats(j)], vs_send.at[t, k], vs_recv.at[t, j],
            r, q * ratio + (j + k) % ratio,
        )

    def vs_in(t, k):
        at = (j + k) % ratio
        spot = vr.at[t, seats(at)]
        return pltpu.make_async_copy(spot, spot, vs_recv.at[t, at])

    def vs_keep(t):
        return pltpu.make_async_copy(vt.at[t], vr.at[t, seats(j)], vl_sem.at[t])

    def v_each(t, act):
        for i in range(1, links):
            if t in DIRECT:
                act(v_out(t, i))
            else:
                @pl.when((q + i) % links != r)
                def _():
                    act(v_out(t, i))
        if t in DIRECT:
            for k in range(1, ratio):
                act(v_side(t, 0, k))
        else:
            @pl.when(aside)
            def _():
                for k in range(1, ratio):
                    act(v_side(t, 0, k))

    def v_direct(t):
        for i in range(1, links):
            v_in(t, ((q + i) % links) * ratio + j).wait()
            for k in range(1, ratio):
                v_side(t, i, k).start()
        for i in range(links):
            for k in range(1, ratio):
                v_in(t, ((q + i) % links) * ratio + (j + k) % ratio).wait()

    closed, gathered = set(), set()

    def v_gather(t):
        if t in DIRECT:
            v_direct(t)
            return

        gathered.add(t)

        @pl.when(aside)
        def _():
            v_direct(t)

        @pl.when(source)
        def _():
            if t not in closed:
                vt_arrive(t)
            vs_keep(t).start()
            for k in range(1, ratio):
                vs_out(t, k).start()
            for k in range(1, ratio):
                vs_in(t, k).wait()
            vs_keep(t).wait()

    def vt_spread(t):
        @pl.when(stays)
        def _():
            vt_in(t).wait()

        @pl.when(jnp.logical_not(stays))
        def _():
            vt_move(t).wait()

        for i in range(1, nrow):
            vt_out(t, i).start()

    def vt_arrive(t):
        for i in range(1, nrow):
            vt_got(t, (r + i) % nrow).wait()

    def vt_close(t):
        if t in gathered:
            @pl.when(aside)
            def _():
                vt_arrive(t)
        else:
            vt_arrive(t)
            closed.add(t)
        vtt[t] = vt[t].astype(jnp.float32).T.astype(jnp.bfloat16)

    def rs_out(t, i):
        peer = (r + i) % nrow
        return remote(
            sent.at[t, peer], got.at[t, r], rs_send.at[t, i], rs_recv.at[t, r], peer, c
        )

    def rs_in(t, peer):
        return pltpu.make_async_copy(sent.at[t, peer], got.at[t, peer], rs_recv.at[t, peer])

    def wc_out(t, i):
        spot = wcc.at[t, r]
        return remote(spot, spot, wc_send.at[t, i], wc_recv.at[t, r], (r + i) % nrow, c)

    def wc_in(t, peer):
        spot = wcc.at[t, peer]
        return pltpu.make_async_copy(spot, spot, wc_recv.at[t, peer])

    def wr_out(t, i):
        return remote(
            wcc.at[t, r], wrc.at[t, j, r], wr_send.at[t, i], wr_recv.at[t, r],
            q, ((q + i) % links) * ratio + j,
        )

    def wr_in(t, peer):
        spot = wrc.at[t, j, peer]
        return pltpu.make_async_copy(spot, spot, wr_recv.at[t, peer])

    def wr_keep(t):
        return pltpu.make_async_copy(wcc.at[t], wrc.at[t, j], local_sem.at[t])

    def wx_out(t, k):
        spot = wrc.at[t, j]
        return remote(
            spot, spot, wx_send.at[t, k], wx_recv.at[t, j], r, q * ratio + (j + k) % ratio
        )

    def wx_in(t, k):
        at = (j + k) % ratio
        spot = wrc.at[t, at]
        return pltpu.make_async_copy(spot, spot, wx_recv.at[t, at])

    def partial(t):
        v_gather(t)
        part[t] = fold(dot(vr[t], ab[...], TN))
        for i in range(1, nrow):
            peer = (r + i) % nrow
            encode(sent.at[t, peer], part[t, strips(peer)])
            rs_out(t, i).start()

    def collect(t):
        total = part[t, strips(r)]
        for i in range(1, nrow):
            peer = (r + i) % nrow
            rs_in(t, peer).wait()
            total = total + decode(got.at[t, peer], strip)
        total = total * scaling
        encode(wcc.at[t, r], total)
        own[t, 0], own[t, 1] = halves(total)

    def spread(t):
        for i in range(1, nrow):
            wc_out(t, i).start()
        for i in range(1, links):
            wr_out(t, i).start()

    def relay(t):
        for i in range(1, nrow):
            wc_in(t, (r + i) % nrow).wait()

        @pl.when(source)
        def _():
            wr_keep(t).start()
            wr_keep(t).wait()

        @pl.when(jnp.logical_not(source))
        def _():
            for i in range(nrow):
                wr_in(t, (r + i) % nrow).wait()

        for k in range(1, ratio):
            wx_out(t, k).start()

    def open_cols(t):
        for k in range(nrow):
            at = pl.ds(k * strip, strip)
            wct[t, 0, at], wct[t, 1, at] = halves(decode(wcc.at[t, k], strip))

    def open_rows(t):
        for k in range(1, ratio):
            wx_in(t, k).wait()
        for s in range(ratio):
            x = jnp.concatenate([decode(wrc.at[t, s, k], strip) for k in range(nrow)], axis=0)
            at = pl.ds(s * cols_tile, cols_tile)
            wr[t, 0, at], wr[t, 1, at] = halves(x.T)

    def ga_out(k, s):
        to = (j + s) % ratio
        return remote(
            gp.at[k, :, thins(to)], ga.at[k, j], ga_send.at[k, s], ga_recv.at[k, j],
            r, q * ratio + to,
        )

    def ga_in(k, s):
        at = (j + s) % ratio
        return pltpu.make_async_copy(ga.at[k, at], ga.at[k, at], ga_recv.at[k, at])

    def gb_out(k, s):
        far = 2**s
        to = q + far - 2 * far * ((q // far) % 2)
        return remote(
            gs.at[k, s], gc.at[k, s], gb_send.at[k, s], gb_recv.at[k, s], r, to * ratio + j
        )

    def gb_in(k, s):
        return pltpu.make_async_copy(gc.at[k, s], gc.at[k, s], gb_recv.at[k, s])

    def gd_out(k, i):
        spot = gq.at[k, j, r]
        return remote(spot, spot, gd_send.at[k, i], gd_recv.at[k, r], (r + i) % nrow, c)

    def gd_in(k, i):
        at = (r + i) % nrow
        spot = gq.at[k, j, at]
        return pltpu.make_async_copy(spot, spot, gd_recv.at[k, at])

    def ge_out(k, s):
        spot = gq.at[k, j]
        return remote(
            spot, spot, ge_send.at[k, s], ge_recv.at[k, j], r, q * ratio + (j + s) % ratio
        )

    def ge_in(k, s):
        at = (j + s) % ratio
        spot = gq.at[k, at]
        return pltpu.make_async_copy(spot, spot, ge_recv.at[k, at])

    def gram_a(k):
        for m, (u, t) in enumerate(chosen):
            gp[k, m] = dot4(own.at[u], vt[t], NN) if k else dot(vtt[u, strips(r)], vt[t], NN)
        for s in range(1, ratio):
            ga_out(k, s).start()

    def gram_b(k):
        for s in range(1, ratio):
            ga_in(k, s).wait()
        totals = []
        for m in range(pairs):
            total = gp[k, m, thins(j)]
            for s in range(1, ratio):
                total = total + ga[k, (j + s) % ratio, m]
            gt[k, m] = total
            totals.append(total)
        encode_all(gs.at[k, 0], totals)
        gb_out(k, 0).start()

    def gram_add(k, s):
        gb_in(k, s).wait()
        totals = []
        for m in range(pairs):
            total = gt[k, m] + decode(gc.at[k, s], thin, m * thin)
            gt[k, m] = total
            totals.append(total)
        return totals

    def gram_c(k):
        for s in range(1, steps):
            encode_all(gs.at[k, s], gram_add(k, s - 1))
            gb_out(k, s).start()

    def gram_d(k):
        encode_all(gq.at[k, j, r], gram_add(k, steps - 1))
        for i in range(1, nrow):
            gd_out(k, i).start()

    def gram_e(k):
        for i in range(1, nrow):
            gd_in(k, i).wait()
        for s in range(1, ratio):
            ge_out(k, s).start()

    def gram_f(k):
        for s in range(1, ratio):
            ge_in(k, s).wait()
        for m in range(pairs):
            for i in range(nrow):
                for s in range(ratio):
                    at = pl.ds(i * strip + s * thin, thin)
                    gram[k, m, at] = decode(gq.at[k, s, i], thin, m * thin)

    def times(k, m, x):
        y = dot(fact[k, m].reshape(2 * depth, depth), x, NN)
        return y[:depth] + y[depth:]

    def keep(k, m, x):
        fact[k, m, 0], fact[k, m, 1] = halves(x)

    def kept(k, m):
        return fact[k, m, 0], fact[k, m, 1]

    def make_c():
        keep(0, 0, -fix * gram[0, 0])
        keep(0, 2, -fix * gram[0, 2])
        keep(0, 1, dot2(kept(0, 0), kept(0, 2), NN) - fix * gram[0, 1])

    def make_d():
        keep(1, 0, -fix * gram[1, 0])
        keep(1, 1, dot2(kept(1, 0), kept(0, 2), NN) - fix * gram[1, 1])
        last = (
            gram[1, 2]
            + dot2(kept(0, 0), halves(gram[1, 1]), TN)
            + dot2(kept(1, 0), halves(gram[0, 1]), TN)
        )
        keep(1, 2, -fix * last)

    def both(x):
        return x[0], x[1]

    def full(x):
        return x[0].astype(jnp.float32) + x[1].astype(jnp.float32)

    def make_z():
        zt[0, 0], zt[0, 1] = halves(
            vtt[0].astype(jnp.float32)
            + times(0, 0, vtt[1]) + times(0, 1, vtt[2])
        )
        zt[1, 0], zt[1, 1] = halves(vtt[1].astype(jnp.float32) + times(0, 2, vtt[2]))

    def minus(terms):
        out_ref[...] = out_ref[...] - half * terms


    vt_start(1)
    vt_start(2)
    a_in.wait()
    ab[...] = wide(halves(a_ref[...]))
    out_ref[...] = a_ref[...]
    vt_start(0)
    v_each(1, start)
    v_each(2, start)
    vt_spread(1)
    vt_spread(2)
    vt_spread(0)
    v_each(0, start)
    partial(1)
    vt_close(1)
    partial(2)
    partial(0)
    vt_close(0)
    vt_close(2)
    gram_a(0)
    gram_b(0)
    collect(1)
    spread(1)
    collect(0)
    gram_a(1)
    gram_c(0)
    gram_b(1)
    collect(2)
    spread(0)
    gram_c(1)
    relay(1)
    gram_d(0)
    open_rows(1)
    spread(2)
    relay(0)
    gram_d(1)
    gram_e(0)
    gram_f(0)
    make_c()
    open_rows(0)
    make_z()
    relay(2)
    open_cols(1)
    open_cols(2)
    open_cols(0)
    minus(fold(dot(wr[1, 0], wide(both(zt.at[1])), NN)) + dot(wr[1, 1], zt[1, 0], NN))
    part[1] = full(wct.at[1]) + dot2(kept(0, 0), both(wct.at[0]), TN)
    part[2] = (
        full(wct.at[2]) + dot2(kept(0, 1), both(wct.at[0]), TN)
        + dot2(kept(0, 2), both(wct.at[1]), TN)
    )
    gram_e(1)
    open_rows(2)
    minus(fold(dot(wr[0, 0], wide(both(zt.at[0])), NN)) + dot(wr[0, 1], zt[0, 0], NN))
    for t in range(ticks):
        v_each(t, wait_send)
        for i in range(1, links):
            wr_out(t, i).wait_send()
        for k in range(1, ratio):
            if t in DIRECT:
                for i in range(1, links):
                    v_side(t, i, k).wait_send()
            else:
                @pl.when(aside)
                def _():
                    for i in range(1, links):
                        v_side(t, i, k).wait_send()

                @pl.when(source)
                def _():
                    vs_out(t, k).wait_send()
        for i in range(1, nrow):
            vt_out(t, i).wait_send()
            rs_out(t, i).wait_send()
            wc_out(t, i).wait_send()

    for k in range(2):
        for s in range(1, ratio):
            ga_out(k, s).wait_send()
        for s in range(steps):
            gb_out(k, s).wait_send()
        for i in range(1, nrow):
            gd_out(k, i).wait_send()

    gram_f(1)
    make_d()
    zero = full(wct.at[0]) + times(1, 0, vtt[1]) + times(1, 1, vtt[2])
    minus(fold(dot(vr[0], wide(halves(zero)), NN)))
    one = part[1] + dot4(kept(1, 0), vtt[0], TN) + times(1, 2, vtt[2])
    minus(fold(dot(vr[1], wide(halves(one)), NN)))
    two = part[2] + dot4(kept(1, 1), vtt[0], TN) + dot4(kept(1, 2), vtt[1], TN)
    minus(fold(dot(vr[2], wide(halves(two)), NN)))
    minus(dot4(both(wr.at[2]), vtt[2], NN))
    mine = rows(c)
    for t in range(ticks):
        total = wr[t, 0, mine].astype(jnp.float32) + wr[t, 1, mine].astype(jnp.float32)
        for m, (u, later) in enumerate(chosen):
            if later == t:
                total = total + dot2((wr[u, 0, mine], wr[u, 1, mine]), kept(0, m), NN)
                total = total + dot3(vr[u, mine], kept(1, m), NN)
        w_ref[t] = total

    for t in range(ticks):
        for k in range(1, ratio):
            wx_out(t, k).wait_send()
    for k in range(2):
        for s in range(1, ratio):
            ge_out(k, s).wait_send()


def on_device(trailing, v_panels):
    nrow = lax.axis_size("row")
    ncol = lax.axis_size("col")
    rows_tile, cols_tile = trailing.shape
    ticks, piece, depth = v_panels.shape
    ratio = rows_tile // cols_tile
    links = ncol // ratio
    scaling = 1.0 / math.sqrt(rows_tile * nrow)
    pairs = ticks * (ticks - 1) // 2
    strip = depth // nrow
    thin = strip // ratio
    steps = links.bit_length() - 1
    dma = pltpu.SemaphoreType.DMA
    vmem = pl.BlockSpec(memory_space=pltpu.VMEM)
    f32, bf16 = jnp.float32, jnp.bfloat16
    return pl.pallas_call(
        functools.partial(kernel, nrow, ncol, ratio, scaling),
        out_shape=(
            jax.ShapeDtypeStruct(trailing.shape, f32),
            jax.ShapeDtypeStruct(v_panels.shape, f32),
        ),
        in_specs=[pl.BlockSpec(memory_space=pltpu.MemorySpace.HBM)] * 2,
        out_specs=(vmem, vmem),
        scratch_shapes=[
            pltpu.VMEM((rows_tile, cols_tile), f32),
            pltpu.VMEM((rows_tile, 2 * cols_tile), bf16),
            pltpu.VMEM((ticks, piece, depth), bf16),
            pltpu.VMEM((ticks, rows_tile, depth), bf16),
            pltpu.VMEM((ticks, cols_tile, depth), bf16),
            pltpu.VMEM((ticks, depth, cols_tile), bf16),
            pltpu.VMEM((ticks, depth, cols_tile), f32),
            pltpu.VMEM((ticks, nrow, strip + TILE, cols_tile), bf16),
            pltpu.VMEM((ticks, nrow, strip + TILE, cols_tile), bf16),
            pltpu.VMEM((ticks, 2, strip, cols_tile), bf16),
            pltpu.VMEM((ticks, nrow, strip + TILE, cols_tile), bf16),
            pltpu.VMEM((ticks, ratio, nrow, strip + TILE, cols_tile), bf16),
            pltpu.VMEM((ticks, 2, depth, cols_tile), bf16),
            pltpu.VMEM((ticks, 2, rows_tile, depth), bf16),
            pltpu.VMEM((ticks - 1, 2, depth, cols_tile), bf16),
            pltpu.VMEM((2, pairs, strip, depth), f32),
            pltpu.VMEM((2, pairs, thin, depth), f32),
            pltpu.VMEM((2, ratio, pairs, thin, depth), f32),
            pltpu.VMEM((2, steps, pairs * thin + TILE, depth), bf16),
            pltpu.VMEM((2, steps, pairs * thin + TILE, depth), bf16),
            pltpu.VMEM((2, ratio, nrow, pairs * thin + TILE, depth), bf16),
            pltpu.VMEM((2, pairs, depth, depth), f32),
            pltpu.VMEM((2, pairs, 2, depth, depth), bf16),
            dma((ticks, links)),
            dma((ticks, ncol)),
            dma((ticks,)),
            dma((ticks,)),
            dma((ticks, links, ratio)),
            dma((ticks, nrow)),
            dma((ticks, nrow)),
            dma((ticks, ratio)),
            dma((ticks, ratio)),
            dma((ticks,)),
            dma((ticks, nrow)),
            dma((ticks, nrow)),
            dma((ticks, nrow)),
            dma((ticks, nrow)),
            dma((ticks, links)),
            dma((ticks, nrow)),
            dma((ticks, ratio)),
            dma((ticks, ratio)),
            dma((ticks,)),
            dma((3,)),
            dma((2, ratio)), dma((2, ratio)),
            dma((2, steps)), dma((2, steps)),
            dma((2, nrow)), dma((2, nrow)),
            dma((2, ratio)), dma((2, ratio)),
        ],
        compiler_params=pltpu.CompilerParams(
            collective_id=0, has_side_effects=True, vmem_limit_bytes=48 * 1024 * 1024
        ),
    )(trailing, v_panels)


def solution(mesh):
    in_specs = (P("row", "col"), P(None, ("row", "col"), None))
    out_specs = (P("row", "col"), P(None, ("row", "col"), None))
    return jax.shard_map(
        on_device, mesh=mesh, in_specs=in_specs, out_specs=out_specs, check_vma=False
    )
```

```python
import functools
import math

import jax
import jax.numpy as jnp
from jax import lax
from jax.experimental import pallas as pl
from jax.experimental.pallas import tpu as pltpu
from jax.sharding import PartitionSpec as P

MESH = pl.DeviceIdType.MESH
NT = (((1,), (1,)), ((), ()))
NN = (((1,), (0,)), ((), ()))
TN = (((0,), (0,)), ((), ()))
SPAN = 124.0
TINY = 1e-30
TILE = 8
DIRECT = ()


def dot(a, b, dims):
    return lax.dot_general(a, b, dims, preferred_element_type=jnp.float32)


def halves(x):
    high = x.astype(jnp.bfloat16)
    return high, (x - high.astype(jnp.float32)).astype(jnp.bfloat16)


def dot2(a, b, dims):
    return dot(a[0], b[0], dims) + (dot(a[0], b[1], dims) + dot(a[1], b[0], dims))


def dot3(a, b, dims):
    return dot(a, b[0], dims) + dot(a, b[1], dims)


def dot4(a, b, dims):
    return dot(a[0], b, dims) + dot(a[1], b, dims)


def fold(x):
    width = x.shape[1] // 2
    return x[:, :width] + x[:, width:]


def wide(pair):
    return jnp.concatenate(pair, axis=1)


def encode(ref, x):
    rows = x.shape[0]
    peak = jnp.maximum(jnp.max(jnp.abs(x), axis=0, keepdims=True), TINY).astype(jnp.bfloat16)
    ref[pl.ds(0, rows)] = jnp.exp2(x * (SPAN / peak.astype(jnp.float32))).astype(jnp.bfloat16)
    ref[pl.ds(ref.shape[0] - TILE, TILE)] = jnp.broadcast_to(peak, (TILE, x.shape[1]))


def encode_all(ref, parts):
    rows = parts[0].shape[0]
    peak = jnp.max(jnp.abs(parts[0]), axis=0, keepdims=True)
    for x in parts[1:]:
        peak = jnp.maximum(peak, jnp.max(jnp.abs(x), axis=0, keepdims=True))
    peak = jnp.maximum(peak, TINY).astype(jnp.bfloat16)
    scale = SPAN / peak.astype(jnp.float32)
    for i, x in enumerate(parts):
        ref[pl.ds(i * rows, rows)] = jnp.exp2(x * scale).astype(jnp.bfloat16)
    ref[pl.ds(ref.shape[0] - TILE, TILE)] = jnp.broadcast_to(peak, (TILE, peak.shape[1]))


def decode(ref, rows, at=0):
    peak = ref[pl.ds(ref.shape[0] - TILE, TILE)].astype(jnp.float32)[:1]
    return jnp.log2(ref[pl.ds(at, rows)].astype(jnp.float32)) * (peak * (1.0 / SPAN))


def kernel(
    nrow, ncol, ratio, scaling,
    a_hbm, v_ref, out_ref, w_ref,
    a_ref, ab, vo, vr, vt, vtt, part, sent, got, own, wcc, wrc, wct, wr, zt, gp, gt, ga, gs, gc, gq, gram, fact,
    v_send, v_recv, vt_send, vt_recv, vx_send, vo_send, vx_recv, vs_send, vs_recv, vl_sem,
    rs_send, rs_recv, wc_send, wc_recv, wr_send, wr_recv, wx_send, wx_recv, local_sem, in_sem,
    ga_send, ga_recv, gb_send, gb_recv, gd_send, gd_recv, ge_send, ge_recv,
):
    ticks, piece, depth = v_ref.shape
    rows_tile, cols_tile = a_hbm.shape
    links = ncol // ratio
    chosen = [(u, t) for t in range(ticks) for u in range(t)]
    pairs = len(chosen)
    r = lax.axis_index("row")
    c = lax.axis_index("col")
    q = c // ratio
    j = c % ratio
    half = 0.5 * scaling
    fix = scaling * half
    strip = depth // nrow
    thin = strip // ratio
    steps = gs.shape[1]

    def rows(at):
        return pl.ds(pl.multiple_of(at * piece, piece), piece)

    def strips(at):
        return pl.ds(pl.multiple_of(at * strip, strip), strip)

    def thins(at):
        return pl.ds(pl.multiple_of(at * thin, thin), thin)

    def remote(src, dst, send, recv, row, col):
        return pltpu.make_async_remote_copy(
            src_ref=src, dst_ref=dst, send_sem=send, recv_sem=recv,
            device_id=(row, col), device_id_type=MESH,
        )

    from_row, from_col = c // ratio, j * nrow + r
    to_row, to_col = c % nrow, r * ratio + c // nrow
    stays = jnp.logical_and(to_row == r, to_col == c)

    a_in = pltpu.make_async_copy(a_hbm, a_ref, in_sem.at[0])
    v_own = pltpu.make_async_copy(v_ref, vr.at[:, rows(c)], in_sem.at[1])
    v_src = pltpu.make_async_copy(v_ref, vo, in_sem.at[2])
    v_src.start()
    v_own.start()
    a_in.start()
    barrier = pltpu.get_barrier_semaphore()

    def greet(row, col):
        pl.semaphore_signal(barrier, inc=1, device_id=(row, col), device_id_type=MESH)

    for i in range(1, nrow):
        greet((r + i) % nrow, c)
    for k in range(1, ratio):
        greet(r, q * ratio + (j + k) % ratio)
    for i in range(1, links):
        greet(r, ((q + i) % links) * ratio + j)

    @pl.when(jnp.logical_not(stays))
    def _():
        greet(from_row, from_col)
        greet(to_row, to_col)

    v_src.wait()
    v_own.wait()
    pl.semaphore_wait(barrier, nrow + ratio + links - 3 + jnp.where(stays, 0, 2))

    def start(copy):
        copy.start()

    def wait_send(copy):
        copy.wait_send()

    def v_out(t, i):
        return remote(
            vo.at[t], vr.at[t, rows(c)], v_send.at[t, i], v_recv.at[t, c],
            r, ((q + i) % links) * ratio + j,
        )

    def v_side(t, i, k):
        at = ((q + i) % links) * ratio + j
        spot = vr.at[t, rows(at)]
        return remote(
            spot if i else vo.at[t], spot, vx_send.at[t, i, k - 1], v_recv.at[t, at],
            r, q * ratio + (j + k) % ratio,
        )

    def v_in(t, col):
        spot = vr.at[t, rows(col)]
        return pltpu.make_async_copy(spot, spot, v_recv.at[t, col])

    def vt_move(t):
        return remote(
            vo.at[t], vt.at[t, rows(to_row)], vt_send.at[t], vt_recv.at[t], to_row, to_col
        )

    def vt_in(t):
        return pltpu.make_async_copy(vo.at[t], vt.at[t, rows(r)], vt_recv.at[t])

    def vt_start(t):
        @pl.when(stays)
        def _():
            vt_in(t).start()

        @pl.when(jnp.logical_not(stays))
        def _():
            vt_move(t).start()

    def vt_out(t, i):
        peer = (r + i) % nrow
        spot = vt.at[t, rows(r)]
        return remote(spot, spot, vo_send.at[t, i], vx_recv.at[t, r], peer, c)

    def vt_got(t, peer):
        spot = vt.at[t, rows(peer)]
        return pltpu.make_async_copy(spot, spot, vx_recv.at[t, peer])

    source = q == r
    aside = jnp.logical_not(source)

    def seats(at):
        return pl.ds(pl.multiple_of(at * cols_tile, cols_tile), cols_tile)

    def vs_out(t, k):
        return remote(
            vt.at[t], vr.at[t, seats(j)], vs_send.at[t, k], vs_recv.at[t, j],
            r, q * ratio + (j + k) % ratio,
        )

    def vs_in(t, k):
        at = (j + k) % ratio
        spot = vr.at[t, seats(at)]
        return pltpu.make_async_copy(spot, spot, vs_recv.at[t, at])

    def vs_keep(t):
        return pltpu.make_async_copy(vt.at[t], vr.at[t, seats(j)], vl_sem.at[t])

    def v_each(t, act):
        for i in range(1, links):
            if t in DIRECT:
                act(v_out(t, i))
            else:
                @pl.when((q + i) % links != r)
                def _():
                    act(v_out(t, i))
        if t in DIRECT:
            for k in range(1, ratio):
                act(v_side(t, 0, k))
        else:
            @pl.when(aside)
            def _():
                for k in range(1, ratio):
                    act(v_side(t, 0, k))

    def v_direct(t):
        for i in range(1, links):
            v_in(t, ((q + i) % links) * ratio + j).wait()
            for k in range(1, ratio):
                v_side(t, i, k).start()
        for i in range(links):
            for k in range(1, ratio):
                v_in(t, ((q + i) % links) * ratio + (j + k) % ratio).wait()

    closed, gathered = set(), set()

    def v_gather(t):
        if t in DIRECT:
            v_direct(t)
            return

        gathered.add(t)

        @pl.when(aside)
        def _():
            v_direct(t)

        @pl.when(source)
        def _():
            if t not in closed:
                vt_arrive(t)
            vs_keep(t).start()
            for k in range(1, ratio):
                vs_out(t, k).start()
            for k in range(1, ratio):
                vs_in(t, k).wait()
            vs_keep(t).wait()

    def vt_spread(t):
        @pl.when(stays)
        def _():
            vt_in(t).wait()

        @pl.when(jnp.logical_not(stays))
        def _():
            vt_move(t).wait()

        for i in range(1, nrow):
            vt_out(t, i).start()

    def vt_arrive(t):
        for i in range(1, nrow):
            vt_got(t, (r + i) % nrow).wait()

    def vt_close(t):
        if t in gathered:
            @pl.when(aside)
            def _():
                vt_arrive(t)
        else:
            vt_arrive(t)
            closed.add(t)
        vtt[t] = vt[t].astype(jnp.float32).T.astype(jnp.bfloat16)

    def rs_out(t, i):
        peer = (r + i) % nrow
        return remote(
            sent.at[t, peer], got.at[t, r], rs_send.at[t, i], rs_recv.at[t, r], peer, c
        )

    def rs_in(t, peer):
        return pltpu.make_async_copy(sent.at[t, peer], got.at[t, peer], rs_recv.at[t, peer])

    def wc_out(t, i):
        spot = wcc.at[t, r]
        return remote(spot, spot, wc_send.at[t, i], wc_recv.at[t, r], (r + i) % nrow, c)

    def wc_in(t, peer):
        spot = wcc.at[t, peer]
        return pltpu.make_async_copy(spot, spot, wc_recv.at[t, peer])

    def wr_out(t, i):
        return remote(
            wcc.at[t, r], wrc.at[t, j, r], wr_send.at[t, i], wr_recv.at[t, r],
            q, ((q + i) % links) * ratio + j,
        )

    def wr_in(t, peer):
        spot = wrc.at[t, j, peer]
        return pltpu.make_async_copy(spot, spot, wr_recv.at[t, peer])

    def wr_keep(t):
        return pltpu.make_async_copy(wcc.at[t], wrc.at[t, j], local_sem.at[t])

    def wx_out(t, k):
        spot = wrc.at[t, j]
        return remote(
            spot, spot, wx_send.at[t, k], wx_recv.at[t, j], r, q * ratio + (j + k) % ratio
        )

    def wx_in(t, k):
        at = (j + k) % ratio
        spot = wrc.at[t, at]
        return pltpu.make_async_copy(spot, spot, wx_recv.at[t, at])

    def partial(t):
        v_gather(t)
        part[t] = fold(dot(vr[t], ab[...], TN))
        for i in range(1, nrow):
            peer = (r + i) % nrow
            encode(sent.at[t, peer], part[t, strips(peer)])
            rs_out(t, i).start()

    def collect(t):
        total = part[t, strips(r)]
        for i in range(1, nrow):
            peer = (r + i) % nrow
            rs_in(t, peer).wait()
            total = total + decode(got.at[t, peer], strip)
        total = total * scaling
        encode(wcc.at[t, r], total)
        own[t, 0], own[t, 1] = halves(total)

    def spread(t):
        for i in range(1, nrow):
            wc_out(t, i).start()
        for i in range(1, links):
            wr_out(t, i).start()

    def relay(t):
        for i in range(1, nrow):
            wc_in(t, (r + i) % nrow).wait()

        @pl.when(source)
        def _():
            wr_keep(t).start()
            wr_keep(t).wait()

        @pl.when(jnp.logical_not(source))
        def _():
            for i in range(nrow):
                wr_in(t, (r + i) % nrow).wait()

        for k in range(1, ratio):
            wx_out(t, k).start()

    def open_cols(t):
        for k in range(nrow):
            at = pl.ds(k * strip, strip)
            wct[t, 0, at], wct[t, 1, at] = halves(decode(wcc.at[t, k], strip))

    def open_rows(t):
        for k in range(1, ratio):
            wx_in(t, k).wait()
        for s in range(ratio):
            x = jnp.concatenate([decode(wrc.at[t, s, k], strip) for k in range(nrow)], axis=0)
            at = pl.ds(s * cols_tile, cols_tile)
            wr[t, 0, at], wr[t, 1, at] = halves(x.T)

    def ga_out(k, s):
        to = (j + s) % ratio
        return remote(
            gp.at[k, :, thins(to)], ga.at[k, j], ga_send.at[k, s], ga_recv.at[k, j],
            r, q * ratio + to,
        )

    def ga_in(k, s):
        at = (j + s) % ratio
        return pltpu.make_async_copy(ga.at[k, at], ga.at[k, at], ga_recv.at[k, at])

    def gb_out(k, s):
        far = 2**s
        to = q + far - 2 * far * ((q // far) % 2)
        return remote(
            gs.at[k, s], gc.at[k, s], gb_send.at[k, s], gb_recv.at[k, s], r, to * ratio + j
        )

    def gb_in(k, s):
        return pltpu.make_async_copy(gc.at[k, s], gc.at[k, s], gb_recv.at[k, s])

    def gd_out(k, i):
        spot = gq.at[k, j, r]
        return remote(spot, spot, gd_send.at[k, i], gd_recv.at[k, r], (r + i) % nrow, c)

    def gd_in(k, i):
        at = (r + i) % nrow
        spot = gq.at[k, j, at]
        return pltpu.make_async_copy(spot, spot, gd_recv.at[k, at])

    def ge_out(k, s):
        spot = gq.at[k, j]
        return remote(
            spot, spot, ge_send.at[k, s], ge_recv.at[k, j], r, q * ratio + (j + s) % ratio
        )

    def ge_in(k, s):
        at = (j + s) % ratio
        spot = gq.at[k, at]
        return pltpu.make_async_copy(spot, spot, ge_recv.at[k, at])

    def gram_a(k):
        for m, (u, t) in enumerate(chosen):
            gp[k, m] = dot4(own.at[u], vt[t], NN) if k else dot(vtt[u, strips(r)], vt[t], NN)
        for s in range(1, ratio):
            ga_out(k, s).start()

    def gram_b(k):
        for s in range(1, ratio):
            ga_in(k, s).wait()
        totals = []
        for m in range(pairs):
            total = gp[k, m, thins(j)]
            for s in range(1, ratio):
                total = total + ga[k, (j + s) % ratio, m]
            gt[k, m] = total
            totals.append(total)
        encode_all(gs.at[k, 0], totals)
        gb_out(k, 0).start()

    def gram_add(k, s):
        gb_in(k, s).wait()
        totals = []
        for m in range(pairs):
            total = gt[k, m] + decode(gc.at[k, s], thin, m * thin)
            gt[k, m] = total
            totals.append(total)
        return totals

    def gram_c(k):
        for s in range(1, steps):
            encode_all(gs.at[k, s], gram_add(k, s - 1))
            gb_out(k, s).start()

    def gram_d(k):
        encode_all(gq.at[k, j, r], gram_add(k, steps - 1))
        for i in range(1, nrow):
            gd_out(k, i).start()

    def gram_e(k):
        for i in range(1, nrow):
            gd_in(k, i).wait()
        for s in range(1, ratio):
            ge_out(k, s).start()

    def gram_f(k):
        for s in range(1, ratio):
            ge_in(k, s).wait()
        for m in range(pairs):
            for i in range(nrow):
                for s in range(ratio):
                    at = pl.ds(i * strip + s * thin, thin)
                    gram[k, m, at] = decode(gq.at[k, s, i], thin, m * thin)

    def times(k, m, x):
        y = dot(fact[k, m].reshape(2 * depth, depth), x, NN)
        return y[:depth] + y[depth:]

    def keep(k, m, x):
        fact[k, m, 0], fact[k, m, 1] = halves(x)

    def kept(k, m):
        return fact[k, m, 0], fact[k, m, 1]

    def make_c():
        keep(0, 0, -fix * gram[0, 0])
        keep(0, 2, -fix * gram[0, 2])
        keep(0, 1, dot2(kept(0, 0), kept(0, 2), NN) - fix * gram[0, 1])

    def make_d():
        keep(1, 0, -fix * gram[1, 0])
        keep(1, 1, dot2(kept(1, 0), kept(0, 2), NN) - fix * gram[1, 1])
        last = (
            gram[1, 2]
            + dot2(kept(0, 0), halves(gram[1, 1]), TN)
            + dot2(kept(1, 0), halves(gram[0, 1]), TN)
        )
        keep(1, 2, -fix * last)

    def both(x):
        return x[0], x[1]

    def full(x):
        return x[0].astype(jnp.float32) + x[1].astype(jnp.float32)

    def make_z():
        zt[0, 0], zt[0, 1] = halves(
            vtt[0].astype(jnp.float32)
            + times(0, 0, vtt[1]) + times(0, 1, vtt[2])
        )
        zt[1, 0], zt[1, 1] = halves(vtt[1].astype(jnp.float32) + times(0, 2, vtt[2]))

    def minus(terms):
        out_ref[...] = out_ref[...] - half * terms


    vt_start(1)
    vt_start(2)
    a_in.wait()
    ab[...] = wide(halves(a_ref[...]))
    out_ref[...] = a_ref[...]
    vt_start(0)
    v_each(1, start)
    v_each(2, start)
    vt_spread(1)
    vt_spread(2)
    vt_spread(0)
    v_each(0, start)
    partial(1)
    vt_close(1)
    partial(2)
    partial(0)
    vt_close(0)
    vt_close(2)
    gram_a(0)
    gram_b(0)
    collect(1)
    spread(1)
    collect(0)
    gram_a(1)
    gram_c(0)
    gram_b(1)
    collect(2)
    spread(0)
    gram_c(1)
    relay(1)
    gram_d(0)
    open_rows(1)
    spread(2)
    relay(0)
    gram_d(1)
    gram_e(0)
    gram_f(0)
    make_c()
    open_rows(0)
    make_z()
    relay(2)
    open_cols(1)
    open_cols(2)
    open_cols(0)
    minus(fold(dot(wr[1, 0], wide(both(zt.at[1])), NN)) + dot(wr[1, 1], zt[1, 0], NN))
    part[1] = full(wct.at[1]) + dot2(kept(0, 0), both(wct.at[0]), TN)
    part[2] = (
        full(wct.at[2]) + dot2(kept(0, 1), both(wct.at[0]), TN)
        + dot2(kept(0, 2), both(wct.at[1]), TN)
    )
    gram_e(1)
    open_rows(2)
    minus(fold(dot(wr[0, 0], wide(both(zt.at[0])), NN)) + dot(wr[0, 1], zt[0, 0], NN))
    for t in range(ticks):
        v_each(t, wait_send)
        for i in range(1, links):
            wr_out(t, i).wait_send()
        for k in range(1, ratio):
            if t in DIRECT:
                for i in range(1, links):
                    v_side(t, i, k).wait_send()
            else:
                @pl.when(aside)
                def _():
                    for i in range(1, links):
                        v_side(t, i, k).wait_send()

                @pl.when(source)
                def _():
                    vs_out(t, k).wait_send()
        for i in range(1, nrow):
            vt_out(t, i).wait_send()
            rs_out(t, i).wait_send()
            wc_out(t, i).wait_send()

    for k in range(2):
        for s in range(1, ratio):
            ga_out(k, s).wait_send()
        for s in range(steps):
            gb_out(k, s).wait_send()
        for i in range(1, nrow):
            gd_out(k, i).wait_send()

    minus(dot4(both(wr.at[2]), vtt[2], NN))
    gram_f(1)
    make_d()
    zero = full(wct.at[0]) + times(1, 0, vtt[1]) + times(1, 1, vtt[2])
    minus(fold(dot(vr[0], wide(halves(zero)), NN)))
    one = part[1] + dot4(kept(1, 0), vtt[0], TN) + times(1, 2, vtt[2])
    minus(fold(dot(vr[1], wide(halves(one)), NN)))
    two = part[2] + dot4(kept(1, 1), vtt[0], TN) + dot4(kept(1, 2), vtt[1], TN)
    minus(fold(dot(vr[2], wide(halves(two)), NN)))
    mine = rows(c)
    for t in range(ticks):
        total = wr[t, 0, mine].astype(jnp.float32) + wr[t, 1, mine].astype(jnp.float32)
        for m, (u, later) in enumerate(chosen):
            if later == t:
                total = total + dot2((wr[u, 0, mine], wr[u, 1, mine]), kept(0, m), NN)
                total = total + dot3(vr[u, mine], kept(1, m), NN)
        w_ref[t] = total

    for t in range(ticks):
        for k in range(1, ratio):
            wx_out(t, k).wait_send()
    for k in range(2):
        for s in range(1, ratio):
            ge_out(k, s).wait_send()


def on_device(trailing, v_panels):
    nrow = lax.axis_size("row")
    ncol = lax.axis_size("col")
    rows_tile, cols_tile = trailing.shape
    ticks, piece, depth = v_panels.shape
    ratio = rows_tile // cols_tile
    links = ncol // ratio
    scaling = 1.0 / math.sqrt(rows_tile * nrow)
    pairs = ticks * (ticks - 1) // 2
    strip = depth // nrow
    thin = strip // ratio
    steps = links.bit_length() - 1
    dma = pltpu.SemaphoreType.DMA
    vmem = pl.BlockSpec(memory_space=pltpu.VMEM)
    f32, bf16 = jnp.float32, jnp.bfloat16
    return pl.pallas_call(
        functools.partial(kernel, nrow, ncol, ratio, scaling),
        out_shape=(
            jax.ShapeDtypeStruct(trailing.shape, f32),
            jax.ShapeDtypeStruct(v_panels.shape, f32),
        ),
        in_specs=[pl.BlockSpec(memory_space=pltpu.MemorySpace.HBM)] * 2,
        out_specs=(vmem, vmem),
        scratch_shapes=[
            pltpu.VMEM((rows_tile, cols_tile), f32),
            pltpu.VMEM((rows_tile, 2 * cols_tile), bf16),
            pltpu.VMEM((ticks, piece, depth), bf16),
            pltpu.VMEM((ticks, rows_tile, depth), bf16),
            pltpu.VMEM((ticks, cols_tile, depth), bf16),
            pltpu.VMEM((ticks, depth, cols_tile), bf16),
            pltpu.VMEM((ticks, depth, cols_tile), f32),
            pltpu.VMEM((ticks, nrow, strip + TILE, cols_tile), bf16),
            pltpu.VMEM((ticks, nrow, strip + TILE, cols_tile), bf16),
            pltpu.VMEM((ticks, 2, strip, cols_tile), bf16),
            pltpu.VMEM((ticks, nrow, strip + TILE, cols_tile), bf16),
            pltpu.VMEM((ticks, ratio, nrow, strip + TILE, cols_tile), bf16),
            pltpu.VMEM((ticks, 2, depth, cols_tile), bf16),
            pltpu.VMEM((ticks, 2, rows_tile, depth), bf16),
            pltpu.VMEM((ticks - 1, 2, depth, cols_tile), bf16),
            pltpu.VMEM((2, pairs, strip, depth), f32),
            pltpu.VMEM((2, pairs, thin, depth), f32),
            pltpu.VMEM((2, ratio, pairs, thin, depth), f32),
            pltpu.VMEM((2, steps, pairs * thin + TILE, depth), bf16),
            pltpu.VMEM((2, steps, pairs * thin + TILE, depth), bf16),
            pltpu.VMEM((2, ratio, nrow, pairs * thin + TILE, depth), bf16),
            pltpu.VMEM((2, pairs, depth, depth), f32),
            pltpu.VMEM((2, pairs, 2, depth, depth), bf16),
            dma((ticks, links)),
            dma((ticks, ncol)),
            dma((ticks,)),
            dma((ticks,)),
            dma((ticks, links, ratio)),
            dma((ticks, nrow)),
            dma((ticks, nrow)),
            dma((ticks, ratio)),
            dma((ticks, ratio)),
            dma((ticks,)),
            dma((ticks, nrow)),
            dma((ticks, nrow)),
            dma((ticks, nrow)),
            dma((ticks, nrow)),
            dma((ticks, links)),
            dma((ticks, nrow)),
            dma((ticks, ratio)),
            dma((ticks, ratio)),
            dma((ticks,)),
            dma((3,)),
            dma((2, ratio)), dma((2, ratio)),
            dma((2, steps)), dma((2, steps)),
            dma((2, nrow)), dma((2, nrow)),
            dma((2, ratio)), dma((2, ratio)),
        ],
        compiler_params=pltpu.CompilerParams(
            collective_id=0, has_side_effects=True, vmem_limit_bytes=48 * 1024 * 1024
        ),
    )(trailing, v_panels)


def solution(mesh):
    in_specs = (P("row", "col"), P(None, ("row", "col"), None))
    out_specs = (P("row", "col"), P(None, ("row", "col"), None))
    return jax.shard_map(
        on_device, mesh=mesh, in_specs=in_specs, out_specs=out_specs, check_vma=False
    )
```
